512 devices in a mesh: member: 2 (over core), gx: 16 (over y, x), gy: 16 (over z).
Axes of the slice: x: 4, y: 4, z: 16, core: 2. Of those that a mesh axis runs over, the one named last changes fastest.
Arguments:
- prior_anomaly_ensemble: float32 [32, 2, 16, 128, 2048], P('member', None, None, 'gx', 'gy'), may hold values from -12 to 12, as said below
- zonal_transport_ratio: float32 [16, 128, 2048], P(None, 'gx', 'gy'), may hold values from -0.25 to 0.25
- meridional_transport_ratio: float32 [16, 128, 2048], P(None, 'gx', 'gy'), may hold values from -0.25 to 0.25
- diffusive_ratio: float32 [16, 128, 2048], P(None, 'gx', 'gy'), may hold values from 0.02 to 0.12
- measured_column_index: int32 [1048576], P(('gx', 'gy')), may hold values from 0 to 262143, as said below
- measured_layer_index: int32 [1048576], P(('gx', 'gy')), may hold values from 0 to 15
- measured_quantity_kind: int32 [1048576], P(('gx', 'gy')), may hold values from 0 to 1
- measured_readings: float32 [1048576], P(('gx', 'gy')), may hold values from -14 to 14
- measured_error_precision: float32 [1048576], P(('gx', 'gy')), may hold values from 7.6293945e-06 to 7.6293945e-05
Outputs:
- analysis: float32 [2, 32, 16, 128, 2048], P('member', None, None, 'gx', 'gy')
The draws below stay inside these ranges and needn't reach their ends.
Inputs may be any that keep to these rules, and one draw needn't show every extreme that they name: `prior_anomaly_ensemble`: the ensemble's initial anomalies. `measured_column_index`: observation o lies in horizontal block o // 4096, blocks of 8 x 128 cells numbered with x blocks slowest; cell = x * 2048 + y.
All inputs are finite; a program needn't handle non-finite values.
Results may differ from the reference program's by a relative error of at most 0.00024.
Values sent between devices are 32-bit elements; how exact they have to be, the bound alone decides.
A program may use at most 64 MiB of HBM per device.

```python
import math
import jax
import jax.numpy as jnp
from jax import lax

M = 32
VARS = 2
LEV = 16
CX = 8
CY = 128
STEPS = 2
OBS_DEV = 4096
NX = 128
NY = 2048
OBS = 1048576


def ensemble_fields(key):
    base = jax.random.fold_in(key, 101)
    field_shape = (M, VARS, LEV, NX, NY)
    return jax.random.truncated_normal(jax.random.fold_in(base, 4), -6.0, 6.0, field_shape, jnp.float32)


def obs_positions(key):
    base = jax.random.fold_in(key, 202)
    index = jnp.arange(OBS, dtype=jnp.int32)
    block = index // OBS_DEV
    blocks_y = NY // CY
    block_x = block // blocks_y
    block_y = block % blocks_y
    pos_x = block_x * CX + jax.random.randint(jax.random.fold_in(base, 1), (OBS,), 0, CX, jnp.int32)
    pos_y = block_y * CY + jax.random.randint(jax.random.fold_in(base, 2), (OBS,), 0, CY, jnp.int32)
    pos_x = jnp.where(index == 0, 0, jnp.where(index == OBS - 1, NX - 1, pos_x))
    pos_y = jnp.where(index == 0, 0, jnp.where(index == OBS - 1, NY - 1, pos_y))
    cell = pos_x * NY + pos_y
    level = jax.random.randint(jax.random.fold_in(base, 3), (OBS,), 0, LEV, jnp.int32)
    level = jnp.where(index == 0, 0, jnp.where(index == 1, LEV - 1, level))
    variable = jax.random.randint(jax.random.fold_in(base, 4), (OBS,), 0, VARS, jnp.int32)
    variable = jnp.where(index == 0, 0, jnp.where(index == 1, VARS - 1, variable))
    return (cell, level, variable)


def draw_prior_anomaly_ensemble(key, part):
    return ensemble_fields(key)


def draw_measured_column_index(key, part):
    return obs_positions(key)[0]


def draw_measured_layer_index(key, part):
    return obs_positions(key)[1]


def draw_measured_quantity_kind(key, part):
    return obs_positions(key)[2]


def draw_measured_readings(key, part):
    fields = ensemble_fields(key)
    cell, level, variable = obs_positions(key)
    truth = jax.random.randint(jax.random.fold_in(key, 303), (), 0, M, jnp.int32)
    picked = fields[truth][variable, level, cell // NY, cell % NY]
    noise_key = jax.random.fold_in(key, 304)
    noise = 0.6 * jax.random.truncated_normal(noise_key, -6.0, 6.0, (OBS,), jnp.float32)
    return 0.8 * picked + noise


def shard_levels(stream_key, extent, pieces, smallest, top_value):
    factor_of = 1.0
    for dim, parts in pieces:
        draws = jax.random.uniform(jax.random.fold_in(jax.random.fold_in(stream_key, 6), dim), (parts,), jnp.float32, smallest / len(pieces), top_value / len(pieces))
        factor_of = factor_of * jnp.repeat(jnp.exp(draws), extent[dim] // parts).reshape((-1,) + (1,) * (len(extent) - 1 - dim))
    return factor_of


def setup_inputs(seed: int = 0) -> dict:
    keys = jax.random.split(jax.random.key(seed), 10)
    return {
        "prior_anomaly_ensemble": draw_prior_anomaly_ensemble(jax.random.fold_in(keys[9], 71), 0),
        "zonal_transport_ratio": jnp.clip(jax.random.uniform(keys[1], (LEV, NX, NY), jnp.float32, -0.25, 0.25) * shard_levels(keys[1], (LEV, NX, NY), ((1, 16), (2, 16)), -0.4, 0.0), -0.25, 0.25),
        "meridional_transport_ratio": jnp.clip(jax.random.uniform(keys[2], (LEV, NX, NY), jnp.float32, -0.25, 0.25) * shard_levels(keys[2], (LEV, NX, NY), ((1, 16), (2, 16)), -0.4, 0.0), -0.25, 0.25),
        "diffusive_ratio": jnp.clip(jnp.exp(math.log(0.12) - 1.7917595 * jax.random.uniform(keys[3], (LEV, NX, NY), jnp.float32) ** shard_levels(keys[3], (LEV, NX, NY), ((1, 16), (2, 16)), -0.2, 0.2)), 0.02, 0.12),
        "measured_column_index": draw_measured_column_index(jax.random.fold_in(keys[9], 71), 0),
        "measured_layer_index": draw_measured_layer_index(jax.random.fold_in(keys[9], 71), 0),
        "measured_quantity_kind": draw_measured_quantity_kind(jax.random.fold_in(keys[9], 71), 0),
        "measured_readings": draw_measured_readings(jax.random.fold_in(keys[9], 71), 0),
        "measured_error_precision": jnp.clip(jnp.exp(math.log(7.62939453125e-05) - 2.3025851 * jax.random.uniform(keys[8], (OBS,), jnp.float32) ** shard_levels(keys[8], (OBS,), ((0, 256),), -0.2, 0.2)), 7.62939453125e-06, 7.62939453125e-05),
    }


def coefficients(zonal_transport_ratio, meridional_transport_ratio, diffusive_ratio):
    east = diffusive_ratio + jnp.maximum(-zonal_transport_ratio, 0.0)
    west = diffusive_ratio + jnp.maximum(zonal_transport_ratio, 0.0)
    north = diffusive_ratio + jnp.maximum(-meridional_transport_ratio, 0.0)
    south = diffusive_ratio + jnp.maximum(meridional_transport_ratio, 0.0)
    return (east, west, north, south)

def advance(padded, east, west, north, south):
    center = padded[..., 1:-1, 1:-1]
    result = center + east * (padded[..., 2:, 1:-1] - center)
    result = result + west * (padded[..., :-2, 1:-1] - center)
    result = result + north * (padded[..., 1:-1, 2:] - center)
    return result + south * (padded[..., 1:-1, :-2] - center)

def transform(gram, drive):
    members = gram.shape[0]
    identity = jnp.eye(members, dtype=gram.dtype)
    system = gram + (members - 1.0) * identity
    factor = jnp.linalg.cholesky(system)
    mean_weights = jax.scipy.linalg.cho_solve((factor, True), drive)
    inverse = jax.scipy.linalg.solve_triangular(factor, identity, lower=True)
    spread = math.sqrt(members - 1.0) * inverse.T
    combined = spread + mean_weights[:, None]
    return combined - lax.optimization_barrier(jnp.mean(combined, axis=0, keepdims=True)) + 1.0 / members

def reference(prior_anomaly_ensemble, zonal_transport_ratio, meridional_transport_ratio, diffusive_ratio, measured_column_index, measured_layer_index, measured_quantity_kind, measured_readings, measured_error_precision):
    east, west, north, south = coefficients(zonal_transport_ratio, meridional_transport_ratio, diffusive_ratio)
    single_realization = prior_anomaly_ensemble
    for step in range(STEPS):
        padded = jnp.pad(single_realization, ((0, 0), (0, 0), (0, 0), (1, 1), (1, 1)))
        single_realization = advance(padded, east, west, north, south)
    cell_x = measured_column_index // NY
    cell_y = measured_column_index % NY
    values = single_realization[:, measured_quantity_kind, measured_layer_index, cell_x, cell_y]
    mean_obs = lax.optimization_barrier(jnp.mean(values, axis=0))
    perturb = values - mean_obs
    innov = measured_readings - mean_obs
    weighted = perturb * measured_error_precision
    gram = jnp.dot(weighted, perturb.T, precision=lax.Precision.HIGHEST)
    drive = jnp.dot(weighted, innov, precision=lax.Precision.HIGHEST)
    mixmat = transform(gram, drive)
    return jnp.einsum('ivlxy,ij->vjlxy', single_realization, mixmat, precision=lax.Precision.HIGHEST)
```

```python
import functools
import math

import jax
import jax.numpy as jnp
from jax import lax
from jax.experimental import pallas as pl
from jax.experimental.pallas import tpu as pltpu
from jax.sharding import PartitionSpec as P

MESH = pl.DeviceIdType.MESH
F32 = jnp.float32
BF16 = jnp.bfloat16
M, LEV, CX, CY = 32, 16, 8, 128
HALF = M // 2
CHUNKS = 4
LC = LEV // CHUNKS
QC = LC // 2
NT = (((1,), (1,)), ((), ()))


def split2(x):
    hi = x.astype(BF16)
    lo = (x - hi.astype(F32)).astype(BF16)
    return hi, lo


def split3(x):
    hi = x.astype(BF16).astype(F32)
    mid = (x - hi).astype(BF16).astype(F32)
    return hi, mid, x - hi - mid


def forecast_kernel(
    prior, zonal, meridional, diffusive, column, layer, kind, readings, precision,
    high_out, low_out, mix_out,
    z0, z1, coef, flow, obs_i, obs_f, hist, weight, packed, west_in, east_in, merged,
    field, high, low, quad, message, plane, line, twin_in,
    local_sem, row_send, row_recv, swap_send, swap_recv, col_send, col_recv,
    row2_send, row2_recv, red_send, red_recv, out_sem,
):
    c = lax.axis_index("member")
    gx = lax.axis_index("gx")
    gy = lax.axis_index("gy")
    other = 1 - c
    mine = pl.multiple_of(c * HALF, HALF)

    local = [pltpu.make_async_copy(prior.at[:, c], z0.at[pl.ds(mine, HALF), :, pl.ds(1, CX), :], local_sem.at[0])]
    for i, ref in enumerate((zonal, meridional, diffusive)):
        local.append(pltpu.make_async_copy(ref, flow.at[i], local_sem.at[1 + i]))
    for i, ref in enumerate((column, layer, kind)):
        local.append(pltpu.make_async_copy(ref, obs_i.at[i], local_sem.at[4 + i]))
    for i, ref in enumerate((readings, precision)):
        local.append(pltpu.make_async_copy(ref, obs_f.at[i], local_sem.at[7 + i]))
    for copy in local:
        copy.start()

    barrier = pltpu.get_barrier_semaphore()
    greet = [(other, gx, gy), (other, (gx + 1) % 16, gy), (other, (gx + 15) % 16, gy)]
    for peer in greet:
        pl.semaphore_signal(barrier, inc=1, device_id=peer, device_id_type=MESH)

    def greet_ring(d, carry):
        pl.semaphore_signal(barrier, inc=1, device_id=(c, (gx + d) % 16, gy), device_id_type=MESH)
        pl.semaphore_signal(barrier, inc=1, device_id=(c, gx, (gy + d) % 16), device_id_type=MESH)
        return carry

    lax.fori_loop(1, 16, greet_ring, 0)
    pl.semaphore_wait(barrier, 33)

    def row_copy(side, variable, k):
        source_row = CX - 1 if side == 0 else 0
        target_row = 0 if side == 0 else CX + 1
        target = gx + 1 if side == 0 else gx - 1
        return pltpu.make_async_remote_copy(
            src_ref=prior.at[:, variable, pl.ds(k * LC, LC), source_row, :],
            dst_ref=z0.at[pl.ds(mine, HALF), pl.ds(k * LC, LC), target_row, :],
            send_sem=row_send.at[side, variable, k],
            recv_sem=row_recv.at[side, c, k],
            device_id=(variable, target, gy),
            device_id_type=MESH,
        )

    def row_arrival(side, source, k):
        target_row = 0 if side == 0 else CX + 1
        here = z0.at[pl.ds(source * HALF, HALF), pl.ds(k * LC, LC), target_row, :]
        return pltpu.make_async_remote_copy(
            src_ref=here, dst_ref=here, send_sem=row_send.at[side, source, k],
            recv_sem=row_recv.at[side, source, k], device_id=(other, gx, gy), device_id_type=MESH,
        )

    def swap_copy(k):
        return pltpu.make_async_remote_copy(
            src_ref=prior.at[:, other, pl.ds(k * LC, LC)],
            dst_ref=z0.at[pl.ds(mine, HALF), pl.ds(k * LC, LC), pl.ds(1, CX), :],
            send_sem=swap_send.at[k], recv_sem=swap_recv.at[k],
            device_id=(other, gx, gy), device_id_type=MESH,
        )

    def swap_arrival(k):
        here = z0.at[pl.ds(pl.multiple_of(other * HALF, HALF), HALF), pl.ds(k * LC, LC), pl.ds(1, CX), :]
        return pltpu.make_async_remote_copy(
            src_ref=here, dst_ref=here, send_sem=swap_send.at[k], recv_sem=swap_recv.at[k],
            device_id=(other, gx, gy), device_id_type=MESH,
        )

    for k in range(CHUNKS):
        swap_copy(k).start()
    for k in range(CHUNKS):
        for variable in range(2):
            @pl.when(gx < 15)
            def _():
                row_copy(0, variable, k).start()

            @pl.when(gx > 0)
            def _():
                row_copy(1, variable, k).start()

    zero_rows = jnp.zeros((M, LEV, CY), F32)
    zero_cols = jnp.zeros((8, CX, CY), F32)

    @pl.when(gx == 0)
    def _():
        z0[:, :, 0, :] = zero_rows
        z1[:, :, 0, :] = zero_rows

    @pl.when(gx == 15)
    def _():
        z0[:, :, CX + 1, :] = zero_rows
        z1[:, :, CX + 1, :] = zero_rows

    @pl.when(gy == 0)
    def _():
        west_in[0] = zero_cols
        west_in[1] = zero_cols

    @pl.when(gy == 15)
    def _():
        east_in[0] = zero_cols
        east_in[1] = zero_cols

    for copy in local[4:]:
        copy.wait()
    cell = obs_i[0]
    spot_a = obs_i[1] * CX + cell // 2048 - gx * CX
    spot_b = cell % 2048 - gy * CY
    kept = jnp.where(obs_i[2] == c, obs_f[1], 0.0)
    obs_i[0] = spot_a
    obs_i[1] = spot_b
    for i, part in enumerate(split3(kept) + split3(kept * obs_f[0])):
        obs_f[2 + i] = part
    hist[...] = jnp.zeros_like(hist)
    rows_iota = lax.broadcasted_iota(jnp.int32, (128, 128), 0)

    def scatter(i, carry):
        lefts, rights = [], []
        for j in range(2):
            r = 2 * i + j
            in_row = rows_iota == obs_i[0, pl.ds(r, 1), :]
            in_col = rows_iota == obs_i[1, pl.ds(r, 1), :]
            lefts.append(jnp.concatenate(
                [jnp.where(in_row, obs_f[2 + p, pl.ds(r, 1), :], 0.0).astype(BF16) for p in range(6)], axis=0))
            rights.append(jnp.where(in_col, 1.0, 0.0).astype(BF16))
        hist[...] += lax.dot_general(
            jnp.concatenate(lefts, axis=1), jnp.concatenate(rights, axis=1), NT, preferred_element_type=F32)
        return carry

    lax.fori_loop(0, 16, scatter, 0)
    for i in range(2):
        base = 384 * i
        total = hist[base:base + 128] + hist[base + 128:base + 256] + hist[base + 256:base + 384]
        weight[i] = total.reshape(LEV, CX, CY)

    for copy in local[1:4]:
        copy.wait()
    zon, mer, dif = flow[0], flow[1], flow[2]
    east = dif + jnp.maximum(-zon, 0.0)
    west = dif + jnp.maximum(zon, 0.0)
    north = dif + jnp.maximum(-mer, 0.0)
    south = dif + jnp.maximum(mer, 0.0)
    coef[0] = 1.0 - (east + west + north + south)
    coef[1] = east
    coef[2] = west
    coef[3] = north
    coef[4] = south

    lanes = lax.broadcasted_iota(jnp.int32, (CX, CY), 1)
    pair = lanes // 2

    def pack(acc, tile, t):
        return jnp.where(pair == t, pltpu.roll(tile, 2 * t + 1, 1), acc)

    def col_copies(stage, first, count, slot):
        out = []
        for side in range(2):
            target = gy + 1 if side == 0 else gy - 1
            into = west_in if side == 0 else east_in
            out.append(pltpu.make_async_remote_copy(
                src_ref=packed.at[stage, pl.ds(first, count)],
                dst_ref=into.at[stage, pl.ds(first, count)],
                send_sem=col_send.at[side, slot], recv_sem=col_recv.at[side, slot],
                device_id=(c, gx, target), device_id_type=MESH,
            ))
        return out

    def guarded(copies, low_ok, high_ok, act):
        for copy, ok in zip(copies, (low_ok, high_ok)):
            @pl.when(ok)
            def _():
                act(copy)

    has_next_y, has_last_y = gy < 15, gy > 0
    has_next_x, has_last_x = gx < 15, gx > 0

    local[0].wait()
    for k in range(CHUNKS):
        swap_arrival(k).wait_recv()

    def pack_first(q, carry):
        acc = jnp.zeros((CX, CY), F32)
        for d in range(2):
            for m in range(M):
                acc = pack(acc, z0[m, 2 * q + d, 1:9, :], d * M + m)
        packed[0, q] = acc
        return carry

    lax.fori_loop(0, 8, pack_first, 0)
    first_cols = col_copies(0, 0, 8, 0)
    guarded(first_cols, has_next_y, has_last_y, lambda copy: copy.start())
    guarded(first_cols, has_last_y, has_next_y, lambda copy: copy.wait_recv())

    odd = lanes % 2 == 1

    def merge(stage, q):
        return jnp.where(odd, pltpu.roll(west_in[stage, q], 1, 1), pltpu.roll(east_in[stage, q], 127, 1))

    def stencil(src, m, l, t, cols, co):
        edge = pltpu.roll(cols, 127 - 2 * t, 1)
        centre = src[m, l, 1:9, :]
        left = jnp.where(lanes == 0, edge, pltpu.roll(centre, 1, 1))
        right = jnp.where(lanes == CY - 1, edge, pltpu.roll(centre, 127, 1))
        return (co[0] * centre + co[1] * src[m, l, 2:10, :] + co[2] * src[m, l, 0:8, :]
                + co[3] * right + co[4] * left)

    def row2_copy(side, k):
        source_row = CX if side == 0 else 1
        target_row = 0 if side == 0 else CX + 1
        target = gx + 1 if side == 0 else gx - 1
        return pltpu.make_async_remote_copy(
            src_ref=z1.at[:, pl.ds(k * LC, LC), source_row, :],
            dst_ref=z1.at[:, pl.ds(k * LC, LC), target_row, :],
            send_sem=row2_send.at[side, k], recv_sem=row2_recv.at[side, k],
            device_id=(c, target, gy), device_id_type=MESH,
        )

    def step_one(q, carry):
        cols = merge(0, q)
        acc = jnp.zeros((CX, CY), F32)
        for d in range(2):
            l = 2 * q + d
            co = [coef[i, l] for i in range(5)]
            for m in range(M):
                new = stencil(z0, m, l, d * M + m, cols, co)
                z1[m, l, 1:9, :] = new
                acc = pack(acc, new, d * M + m)
        packed[1, q] = acc
        return carry

    for k in range(CHUNKS):
        for source in range(2):
            guarded([row_arrival(0, source, k), row_arrival(1, source, k)],
                    has_last_x, has_next_x, lambda copy: copy.wait_recv())
        lax.fori_loop(k * QC, (k + 1) * QC, step_one, 0)
        guarded([row2_copy(0, k), row2_copy(1, k)], has_next_x, has_last_x, lambda copy: copy.start())
        guarded(col_copies(1, k * QC, QC, 1 + k), has_next_y, has_last_y, lambda copy: copy.start())

    quad[...] = jnp.zeros_like(quad)

    def step_two(q, carry):
        cols = merge(1, q)
        lefts, rights = [], []
        for d in range(2):
            l = 2 * q + d
            co = [coef[i, l] for i in range(5)]
            total = jnp.zeros((CX, CY), F32)
            for m in range(M):
                new = stencil(z1, m, l, d * M + m, cols, co)
                field[m * CX:(m + 1) * CX, :] = new
                total = total + new
            mean = total * (1.0 / M)
            state = field[...]
            hi, lo = split2(state)
            high[l] = hi
            low[l] = lo
            part = (state.reshape(M, CX, CY) - mean[None])
            w = weight[0, l]
            rights.append(part.reshape(M * CX, CY))
            innov = weight[1, l] - w * mean
            lefts.append(jnp.concatenate(
                [(part * w[None]).reshape(M * CX, CY), innov, jnp.zeros((CX, CY), F32)], axis=0))
        left_hi, left_lo = split2(jnp.concatenate(lefts, axis=1))
        right_hi, right_lo = split2(jnp.concatenate(rights, axis=1))
        dot = functools.partial(lax.dot_general, dimension_numbers=NT, preferred_element_type=F32)
        quad[...] += dot(left_hi, right_hi) + dot(left_hi, right_lo) + dot(left_lo, right_hi)
        return carry

    for k in range(CHUNKS):
        guarded([row2_copy(0, k), row2_copy(1, k)], has_last_x, has_next_x, lambda copy: copy.wait_recv())
        guarded(col_copies(1, k * QC, QC, 1 + k), has_last_y, has_next_y, lambda copy: copy.wait_recv())
        lax.fori_loop(k * QC, (k + 1) * QC, step_two, 0)

    outs = [pltpu.make_async_copy(high, high_out, out_sem.at[0]), pltpu.make_async_copy(low, low_out, out_sem.at[1])]
    for copy in outs:
        copy.start()

    row_x = lax.broadcasted_iota(jnp.int32, (272, 256), 0) % CX
    col_x = lax.broadcasted_iota(jnp.int32, (272, 256), 1) % CX
    kept_terms = jnp.where(row_x == col_x, quad[...], 0.0)
    fold = (lax.broadcasted_iota(jnp.int32, (256, 128), 0) // CX
            == lax.broadcasted_iota(jnp.int32, (256, 128), 1) % M)
    fold = jnp.where(fold, 1.0, 0.0).astype(BF16)
    summed = sum(jnp.dot(part.astype(BF16), fold, preferred_element_type=F32) for part in split3(kept_terms))
    summed = jnp.sum(summed.reshape(34, CX, 128), axis=1)
    gram = summed[0:M]
    drive = summed[M:M + 1]
    ri = lax.broadcasted_iota(jnp.int32, (M, 128), 0)
    li = lax.broadcasted_iota(jnp.int32, (M, 128), 1)
    ci = li % M
    folded = jnp.where(ci >= ri, gram, jnp.where(ci == ri - 1, drive, 0.0))
    folded = jnp.where((ri == 2) & (ci == 0), pltpu.roll(drive, 1, 1), folded)
    block = lanes // M
    tile = jnp.zeros((8, 128), F32)
    for b in range(4):
        tile = jnp.where(block == b, folded[8 * b:8 * b + 8], tile)

    def gather_sum(stage, buffer, peer_of, tile):
        message[stage] = tile

        def copy_of(d):
            return pltpu.make_async_remote_copy(
                src_ref=message.at[stage], dst_ref=buffer.at[d],
                send_sem=red_send.at[stage, d], recv_sem=red_recv.at[stage, d],
                device_id=peer_of(d), device_id_type=MESH,
            )

        def start(d, carry):
            copy_of(d).start()
            return carry

        def finish(d, carry):
            copy_of(d).wait_recv()
            return carry

        lax.fori_loop(1, 16, start, 0)
        lax.fori_loop(1, 16, finish, 0)
        total = tile
        for d in range(1, 16):
            total = total + buffer[d]
        return total, copy_of

    tile, plane_copy = gather_sum(0, plane, lambda d: (c, (gx + d) % 16, gy), tile)
    tile, line_copy = gather_sum(1, line, lambda d: (c, gx, (gy + d) % 16), tile)
    message[2] = tile
    twin_copy = pltpu.make_async_remote_copy(
        src_ref=message.at[2], dst_ref=twin_in, send_sem=red_send.at[2, 0], recv_sem=red_recv.at[2, 0],
        device_id=(other, gx, gy), device_id_type=MESH)
    twin_copy.start()
    twin_copy.wait_recv()
    tile = tile + twin_in[...]

    square = jnp.concatenate([tile] + [pltpu.roll(tile, 128 - M * b, 1) for b in range(1, 4)], axis=0)
    flipped = jnp.transpose(jnp.concatenate([square, jnp.zeros((96, 128), F32)], axis=0))[0:M]
    upper = li >= ri
    system = jnp.where(upper, square, flipped) + jnp.where(li == ri, M - 1.0, 0.0)
    drive_col = jnp.sum(jnp.where((li == ri + 1), flipped, 0.0), axis=1, keepdims=True)
    last = jnp.sum(jnp.where((ri == 2) & (li == 0), square, 0.0))
    drive_col = jnp.where(ri == M - 1, last, drive_col)
    work = jnp.where(li < M, system, 0.0)
    work = jnp.where(li == ri + M, 1.0, work)
    work = jnp.where(li == 2 * M, drive_col, work)
    pivots = jnp.ones((M, 128), F32)
    for k in range(M):
        row = jnp.broadcast_to(work[k:k + 1, :], (M, 128))
        column_k = jnp.broadcast_to(work[:, k:k + 1], (M, 128))
        pivot = jnp.broadcast_to(work[k:k + 1, k:k + 1], (M, 128))
        pivots = jnp.where(ri == k, pivot, pivots)
        work = work - jnp.where(ri > k, column_k / pivot, 0.0) * row
    scaled = work * lax.rsqrt(pivots)
    inverse = jnp.where((li >= M) & (li < 2 * M), scaled, 0.0)
    reduced = jnp.sum(jnp.where(li == 2 * M, scaled, 0.0), axis=1, keepdims=True)
    mean_weights = jnp.sum(inverse * reduced, axis=0, keepdims=True)
    combined = math.sqrt(M - 1.0) * inverse + mean_weights
    average = jnp.sum(combined, axis=1, keepdims=True) * (1.0 / M)
    mix_out[...] = combined - average + 1.0 / M

    for copy in outs:
        copy.wait()
    for k in range(CHUNKS):
        swap_copy(k).wait_send()
        for variable in range(2):
            guarded([row_copy(0, variable, k), row_copy(1, variable, k)],
                    has_next_x, has_last_x, lambda copy: copy.wait_send())
        guarded([row2_copy(0, k), row2_copy(1, k)], has_next_x, has_last_x, lambda copy: copy.wait_send())
        guarded(col_copies(1, k * QC, QC, 1 + k), has_next_y, has_last_y, lambda copy: copy.wait_send())
    guarded(first_cols, has_next_y, has_last_y, lambda copy: copy.wait_send())

    def drain(d, carry):
        plane_copy(d).wait_send()
        line_copy(d).wait_send()
        return carry

    lax.fori_loop(1, 16, drain, 0)
    twin_copy.wait_send()


def mix_kernel(mix, high, low, out, mix_hi, mix_lo):
    @pl.when(pl.program_id(0) == 0)
    def _():
        spread = (lax.broadcasted_iota(jnp.int32, (128, 256), 0)
                  == lax.broadcasted_iota(jnp.int32, (128, 256), 1) // CX + M)
        spread = jnp.where(spread, 1.0, 0.0).astype(BF16)
        wide = sum(jnp.dot(part.astype(BF16), spread, preferred_element_type=F32) for part in split3(mix[...]))
        wide = jnp.broadcast_to(wide[:, None, :], (M, CX, 256)).reshape(256, 256)
        same = (lax.broadcasted_iota(jnp.int32, (256, 256), 0) % CX
                == lax.broadcasted_iota(jnp.int32, (256, 256), 1) % CX)
        hi, lo = split2(jnp.where(same, wide, 0.0))
        mix_hi[...] = hi
        mix_lo[...] = lo

    hi = jnp.concatenate([high[0], high[1]], axis=1)
    lo = jnp.concatenate([low[0], low[1]], axis=1)
    dot = functools.partial(jnp.dot, preferred_element_type=F32)
    mixed = dot(mix_hi[...], hi) + dot(mix_hi[...], lo) + dot(mix_lo[...], hi)
    for d in range(2):
        out[0, :, d] = mixed[:, d * CY:(d + 1) * CY].reshape(M, CX, CY)


def shards(prior, zonal, meridional, diffusive, column, layer, kind, readings, precision):
    obs = [x.reshape(32, 128) for x in (column, layer, kind, readings, precision)]
    anywhere = pl.BlockSpec(memory_space=pl.ANY)
    high, low, mix = pl.pallas_call(
        forecast_kernel,
        out_shape=(
            jax.ShapeDtypeStruct((LEV, M * CX, CY), BF16),
            jax.ShapeDtypeStruct((LEV, M * CX, CY), BF16),
            jax.ShapeDtypeStruct((M, 128), F32),
        ),
        in_specs=[anywhere] * 9,
        out_specs=(anywhere, anywhere, pl.BlockSpec(memory_space=pltpu.VMEM)),
        scratch_shapes=[
            pltpu.VMEM((M, LEV, CX + 2, CY), F32),
            pltpu.VMEM((M, LEV, CX + 2, CY), F32),
            pltpu.VMEM((5, LEV, CX, CY), F32),
            pltpu.VMEM((3, LEV, CX, CY), F32),
            pltpu.VMEM((3, 32, 128), jnp.int32),
            pltpu.VMEM((8, 32, 128), F32),
            pltpu.VMEM((768, 128), F32),
            pltpu.VMEM((2, LEV, CX, CY), F32),
            pltpu.VMEM((2, 8, CX, CY), F32),
            pltpu.VMEM((2, 8, CX, CY), F32),
            pltpu.VMEM((2, 8, CX, CY), F32),
            pltpu.VMEM((8, 128), F32),
            pltpu.VMEM((M * CX, CY), F32),
            pltpu.VMEM((LEV, M * CX, CY), BF16),
            pltpu.VMEM((LEV, M * CX, CY), BF16),
            pltpu.VMEM((272, 256), F32),
            pltpu.VMEM((3, 8, 128), F32),
            pltpu.VMEM((16, 8, 128), F32),
            pltpu.VMEM((16, 8, 128), F32),
            pltpu.VMEM((8, 128), F32),
            pltpu.SemaphoreType.DMA((9,)),
            pltpu.SemaphoreType.DMA((2, 2, CHUNKS)),
            pltpu.SemaphoreType.DMA((2, 2, CHUNKS)),
            pltpu.SemaphoreType.DMA((CHUNKS,)),
            pltpu.SemaphoreType.DMA((CHUNKS,)),
            pltpu.SemaphoreType.DMA((2, 1 + CHUNKS)),
            pltpu.SemaphoreType.DMA((2, 1 + CHUNKS)),
            pltpu.SemaphoreType.DMA((2, CHUNKS)),
            pltpu.SemaphoreType.DMA((2, CHUNKS)),
            pltpu.SemaphoreType.DMA((3, 16)),
            pltpu.SemaphoreType.DMA((3, 16)),
            pltpu.SemaphoreType.DMA((2,)),
        ],
        compiler_params=pltpu.CompilerParams(collective_id=0, has_side_effects=True),
        name="forecast",
    )(prior, zonal, meridional, diffusive, *obs)
    return pl.pallas_call(
        mix_kernel,
        grid=(LEV // 2,),
        out_shape=jax.ShapeDtypeStruct((1, M, LEV, CX, CY), F32),
        in_specs=[
            pl.BlockSpec((M, 128), lambda i: (0, 0)),
            pl.BlockSpec((2, M * CX, CY), lambda i: (i, 0, 0)),
            pl.BlockSpec((2, M * CX, CY), lambda i: (i, 0, 0)),
        ],
        out_specs=pl.BlockSpec((1, M, 2, CX, CY), lambda i: (0, 0, i, 0, 0)),
        scratch_shapes=[pltpu.VMEM((256, 256), BF16), pltpu.VMEM((256, 256), BF16)],
        name="mix",
    )(mix, high, low)


def solution(mesh):
    obs = P(("gx", "gy"))
    flow = P(None, "gx", "gy")
    return jax.shard_map(
        shards,
        mesh=mesh,
        in_specs=(P("member", None, None, "gx", "gy"), flow, flow, flow, obs, obs, obs, obs, obs),
        out_specs=P("member", None, None, "gx", "gy"),
        check_vma=False,
    )
```

```python
import functools
import math

import jax
import jax.numpy as jnp
from jax import lax
from jax.experimental import pallas as pl
from jax.experimental.pallas import tpu as pltpu
from jax.sharding import PartitionSpec as P

MESH = pl.DeviceIdType.MESH
F32 = jnp.float32
BF16 = jnp.bfloat16
M, LEV, CX, CY = 32, 16, 8, 128
HALF = M // 2
CHUNKS = 4
LC = LEV // CHUNKS
QC = LC // 2
NT = (((1,), (1,)), ((), ()))


def split2(x):
    hi = x.astype(BF16)
    lo = (x - hi.astype(F32)).astype(BF16)
    return hi, lo


def split3(x):
    hi = x.astype(BF16).astype(F32)
    mid = (x - hi).astype(BF16).astype(F32)
    return hi, mid, x - hi - mid


def forecast_kernel(
    prior, zonal, meridional, diffusive, column, layer, kind, readings, precision,
    high, low, mix_out,
    z0, z1, coef, flow, obs_i, obs_f, hist, weight, packed, west_in, east_in,
    field, quad, message, plane, line, twin_in,
    local_sem, row_send, row_recv, swap_send, swap_recv, col_send, col_recv,
    row2_send, row2_recv, red_send, red_recv, news,
):
    c = lax.axis_index("member")
    gx = lax.axis_index("gx")
    gy = lax.axis_index("gy")
    other = 1 - c
    mine = pl.multiple_of(c * HALF, HALF)

    local = [pltpu.make_async_copy(prior.at[:, c], z0.at[pl.ds(mine, HALF), :, pl.ds(1, CX), :], local_sem.at[0])]
    for i, ref in enumerate((zonal, meridional, diffusive)):
        local.append(pltpu.make_async_copy(ref, flow.at[i], local_sem.at[1 + i]))
    for i, ref in enumerate((column, layer, kind)):
        local.append(pltpu.make_async_copy(ref, obs_i.at[i], local_sem.at[4 + i]))
    for i, ref in enumerate((readings, precision)):
        local.append(pltpu.make_async_copy(ref, obs_f.at[i], local_sem.at[7 + i]))
    for copy in local:
        copy.start()

    barrier = pltpu.get_barrier_semaphore()
    def ring_peers(distance):
        return [(c, (gx + distance) % 16, gy), (c, (gx + 16 - distance) % 16, gy),
                (c, gx, (gy + distance) % 16), (c, gx, (gy + 16 - distance) % 16)]

    greet = [(other, gx, gy), (other, (gx + 1) % 16, gy), (other, (gx + 15) % 16, gy)] + ring_peers(1)
    for peer in greet:
        pl.semaphore_signal(barrier, inc=1, device_id=peer, device_id_type=MESH)
    pl.semaphore_wait(barrier, len(greet))

    def tell(stage):
        for peer in ring_peers(2 ** stage):
            pl.semaphore_signal(news.at[stage], inc=1, device_id=peer, device_id_type=MESH)

    def hear(stage):
        pl.semaphore_wait(news.at[stage], 4)

    def row_copy(side, variable, k):
        source_row = CX - 1 if side == 0 else 0
        target_row = 0 if side == 0 else CX + 1
        target = gx + 1 if side == 0 else gx - 1
        return pltpu.make_async_remote_copy(
            src_ref=prior.at[:, variable, pl.ds(k * LC, LC), source_row, :],
            dst_ref=z0.at[pl.ds(mine, HALF), pl.ds(k * LC, LC), target_row, :],
            send_sem=row_send.at[side, variable, k],
            recv_sem=row_recv.at[side, c, k],
            device_id=(variable, target, gy),
            device_id_type=MESH,
        )

    def row_arrival(side, source, k):
        target_row = 0 if side == 0 else CX + 1
        here = z0.at[pl.ds(source * HALF, HALF), pl.ds(k * LC, LC), target_row, :]
        return pltpu.make_async_remote_copy(
            src_ref=here, dst_ref=here, send_sem=row_send.at[side, source, k],
            recv_sem=row_recv.at[side, source, k], device_id=(other, gx, gy), device_id_type=MESH,
        )

    def swap_copy(k):
        return pltpu.make_async_remote_copy(
            src_ref=prior.at[:, other, pl.ds(k * LC, LC)],
            dst_ref=z0.at[pl.ds(mine, HALF), pl.ds(k * LC, LC), pl.ds(1, CX), :],
            send_sem=swap_send.at[k], recv_sem=swap_recv.at[k],
            device_id=(other, gx, gy), device_id_type=MESH,
        )

    def swap_arrival(k):
        here = z0.at[pl.ds(pl.multiple_of(other * HALF, HALF), HALF), pl.ds(k * LC, LC), pl.ds(1, CX), :]
        return pltpu.make_async_remote_copy(
            src_ref=here, dst_ref=here, send_sem=swap_send.at[k], recv_sem=swap_recv.at[k],
            device_id=(other, gx, gy), device_id_type=MESH,
        )

    for k in range(CHUNKS):
        swap_copy(k).start()
    for k in range(CHUNKS):
        for variable in range(2):
            @pl.when(gx < 15)
            def _():
                row_copy(0, variable, k).start()

            @pl.when(gx > 0)
            def _():
                row_copy(1, variable, k).start()

    tell(0)

    zero_rows = jnp.zeros((M, LEV, CY), F32)
    zero_cols = jnp.zeros((8, CX, CY), F32)

    @pl.when(gx == 0)
    def _():
        z0[:, :, 0, :] = zero_rows
        z1[:, :, 0, :] = zero_rows

    @pl.when(gx == 15)
    def _():
        z0[:, :, CX + 1, :] = zero_rows
        z1[:, :, CX + 1, :] = zero_rows

    @pl.when(gy == 0)
    def _():
        west_in[0] = zero_cols
        west_in[1] = zero_cols

    @pl.when(gy == 15)
    def _():
        east_in[0] = zero_cols
        east_in[1] = zero_cols

    for copy in local[4:]:
        copy.wait()
    cell = obs_i[0]
    spot_a = obs_i[1] * CX + cell // 2048 - gx * CX
    spot_b = cell % 2048 - gy * CY
    kept = jnp.where(obs_i[2] == c, obs_f[1], 0.0)
    obs_i[0] = spot_a
    obs_i[1] = spot_b
    for i, part in enumerate(split3(kept) + split3(kept * obs_f[0])):
        obs_f[2 + i] = part
    hist[...] = jnp.zeros_like(hist)
    rows_iota = lax.broadcasted_iota(jnp.int32, (128, 128), 0)

    def scatter(i, carry):
        lefts, rights = [], []
        for j in range(2):
            r = 2 * i + j
            in_row = rows_iota == obs_i[0, pl.ds(r, 1), :]
            in_col = rows_iota == obs_i[1, pl.ds(r, 1), :]
            lefts.append(jnp.concatenate(
                [jnp.where(in_row, obs_f[2 + p, pl.ds(r, 1), :], 0.0).astype(BF16) for p in range(6)], axis=0))
            rights.append(jnp.where(in_col, 1.0, 0.0).astype(BF16))
        hist[...] += lax.dot_general(
            jnp.concatenate(lefts, axis=1), jnp.concatenate(rights, axis=1), NT, preferred_element_type=F32)
        return carry

    lax.fori_loop(0, 8, scatter, 0)
    hear(0)
    tell(1)

    for copy in local[1:4]:
        copy.wait()
    zon, mer, dif = flow[0], flow[1], flow[2]
    east = dif + jnp.maximum(-zon, 0.0)
    west = dif + jnp.maximum(zon, 0.0)
    north = dif + jnp.maximum(-mer, 0.0)
    south = dif + jnp.maximum(mer, 0.0)
    coef[0] = 1.0 - (east + west + north + south)
    coef[1] = east
    coef[2] = west
    coef[3] = north
    coef[4] = south

    lanes = lax.broadcasted_iota(jnp.int32, (CX, CY), 1)
    pair = lanes // 2

    def pack(acc, tile, t):
        return jnp.where(pair == t, pltpu.roll(tile, 2 * t + 1, 1), acc)

    def col_copies(stage, first, count, slot):
        out = []
        for side in range(2):
            target = gy + 1 if side == 0 else gy - 1
            into = west_in if side == 0 else east_in
            out.append(pltpu.make_async_remote_copy(
                src_ref=packed.at[stage, pl.ds(first, count)],
                dst_ref=into.at[stage, pl.ds(first, count)],
                send_sem=col_send.at[side, slot], recv_sem=col_recv.at[side, slot],
                device_id=(c, gx, target), device_id_type=MESH,
            ))
        return out

    def guarded(copies, low_ok, high_ok, act):
        for copy, ok in zip(copies, (low_ok, high_ok)):
            @pl.when(ok)
            def _():
                act(copy)

    has_next_y, has_last_y = gy < 15, gy > 0
    has_next_x, has_last_x = gx < 15, gx > 0

    local[0].wait()
    for k in range(CHUNKS):
        swap_arrival(k).wait_recv()

    def pack_first(q, carry):
        acc = jnp.zeros((CX, CY), F32)
        for d in range(2):
            for m in range(M):
                acc = pack(acc, z0[m, 2 * q + d, 1:9, :], d * M + m)
        packed[0, q] = acc
        return carry

    lax.fori_loop(0, 8, pack_first, 0)
    first_cols = col_copies(0, 0, 8, 0)
    guarded(first_cols, has_next_y, has_last_y, lambda copy: copy.start())
    hear(1)
    tell(2)
    lax.fori_loop(8, 16, scatter, 0)
    for i in range(2):
        base = 384 * i
        total = hist[base:base + 128] + hist[base + 128:base + 256] + hist[base + 256:base + 384]
        weight[i] = total.reshape(LEV, CX, CY)
    hear(2)
    guarded(first_cols, has_last_y, has_next_y, lambda copy: copy.wait_recv())

    odd = lanes % 2 == 1

    def merge(stage, q):
        return jnp.where(odd, pltpu.roll(west_in[stage, q], 1, 1), pltpu.roll(east_in[stage, q], 127, 1))

    def stencil(src, m, l, t, cols, co):
        edge = pltpu.roll(cols, 127 - 2 * t, 1)
        centre = src[m, l, 1:9, :]
        left = jnp.where(lanes == 0, edge, pltpu.roll(centre, 1, 1))
        right = jnp.where(lanes == CY - 1, edge, pltpu.roll(centre, 127, 1))
        return (co[0] * centre + co[1] * src[m, l, 2:10, :] + co[2] * src[m, l, 0:8, :]
                + co[3] * right + co[4] * left)

    def row2_copy(side, k):
        source_row = CX if side == 0 else 1
        target_row = 0 if side == 0 else CX + 1
        target = gx + 1 if side == 0 else gx - 1
        return pltpu.make_async_remote_copy(
            src_ref=z1.at[:, pl.ds(k * LC, LC), source_row, :],
            dst_ref=z1.at[:, pl.ds(k * LC, LC), target_row, :],
            send_sem=row2_send.at[side, k], recv_sem=row2_recv.at[side, k],
            device_id=(c, target, gy), device_id_type=MESH,
        )

    def step_one(q, carry):
        cols = merge(0, q)
        acc = jnp.zeros((CX, CY), F32)
        for d in range(2):
            l = 2 * q + d
            co = [coef[i, l] for i in range(5)]
            for m in range(M):
                new = stencil(z0, m, l, d * M + m, cols, co)
                z1[m, l, 1:9, :] = new
                acc = pack(acc, new, d * M + m)
        packed[1, q] = acc
        return carry

    for k in range(CHUNKS):
        for source in range(2):
            guarded([row_arrival(0, source, k), row_arrival(1, source, k)],
                    has_last_x, has_next_x, lambda copy: copy.wait_recv())
        lax.fori_loop(k * QC, (k + 1) * QC, step_one, 0)
        guarded([row2_copy(0, k), row2_copy(1, k)], has_next_x, has_last_x, lambda copy: copy.start())
        guarded(col_copies(1, k * QC, QC, 1 + k), has_next_y, has_last_y, lambda copy: copy.start())

    quad[...] = jnp.zeros_like(quad)

    def step_two(q, carry):
        cols = merge(1, q)
        lefts, rights = [], []
        for d in range(2):
            l = 2 * q + d
            co = [coef[i, l] for i in range(5)]
            total = jnp.zeros((CX, CY), F32)
            for m in range(M):
                new = stencil(z1, m, l, d * M + m, cols, co)
                field[m * CX:(m + 1) * CX, :] = new
                total = total + new
            mean = total * (1.0 / M)
            state = field[...]
            hi, lo = split2(state)
            high[l] = hi
            low[l] = lo
            part = (state.reshape(M, CX, CY) - mean[None])
            w = weight[0, l]
            rights.append(part.reshape(M * CX, CY))
            innov = weight[1, l] - w * mean
            lefts.append(jnp.concatenate(
                [(part * w[None]).reshape(M * CX, CY), innov, jnp.zeros((CX, CY), F32)], axis=0))
        left_hi, left_lo = split2(jnp.concatenate(lefts, axis=1))
        right_hi, right_lo = split2(jnp.concatenate(rights, axis=1))
        dot = functools.partial(lax.dot_general, dimension_numbers=NT, preferred_element_type=F32)
        quad[...] += dot(left_hi, right_hi) + dot(left_hi, right_lo) + dot(left_lo, right_hi)
        return carry

    for k in range(CHUNKS):
        guarded([row2_copy(0, k), row2_copy(1, k)], has_last_x, has_next_x, lambda copy: copy.wait_recv())
        guarded(col_copies(1, k * QC, QC, 1 + k), has_last_y, has_next_y, lambda copy: copy.wait_recv())
        lax.fori_loop(k * QC, (k + 1) * QC, step_two, 0)

    row_x = lax.broadcasted_iota(jnp.int32, (272, 256), 0) % CX
    col_x = lax.broadcasted_iota(jnp.int32, (272, 256), 1) % CX
    kept_terms = jnp.where(row_x == col_x, quad[...], 0.0)
    fold = (lax.broadcasted_iota(jnp.int32, (256, 128), 0) // CX
            == lax.broadcasted_iota(jnp.int32, (256, 128), 1) % M)
    fold = jnp.where(fold, 1.0, 0.0).astype(BF16)
    summed = sum(jnp.dot(part.astype(BF16), fold, preferred_element_type=F32) for part in split3(kept_terms))
    summed = jnp.sum(summed.reshape(34, CX, 128), axis=1)
    gram = summed[0:M]
    drive = summed[M:M + 1]
    ri = lax.broadcasted_iota(jnp.int32, (M, 128), 0)
    li = lax.broadcasted_iota(jnp.int32, (M, 128), 1)
    ci = li % M
    folded = jnp.where(ci >= ri, gram, jnp.where(ci == ri - 1, drive, 0.0))
    folded = jnp.where((ri == 2) & (ci == 0), pltpu.roll(drive, 1, 1), folded)
    block = lanes // M
    tile = jnp.zeros((8, 128), F32)
    for b in range(4):
        tile = jnp.where(block == b, folded[8 * b:8 * b + 8], tile)

    def gather_sum(stage, buffer, peer_of, tile):
        message[stage] = tile

        def copy_of(d):
            return pltpu.make_async_remote_copy(
                src_ref=message.at[stage], dst_ref=buffer.at[d],
                send_sem=red_send.at[stage, d], recv_sem=red_recv.at[stage, d],
                device_id=peer_of(d), device_id_type=MESH,
            )

        def start(d, carry):
            copy_of(d).start()
            return carry

        def finish(d, carry):
            copy_of(d).wait_recv()
            return carry

        lax.fori_loop(1, 16, start, 0)
        lax.fori_loop(1, 16, finish, 0)
        total = tile
        for d in range(1, 16):
            total = total + buffer[d]
        return total, copy_of

    tile, plane_copy = gather_sum(0, plane, lambda d: (c, (gx + d) % 16, gy), tile)
    tile, line_copy = gather_sum(1, line, lambda d: (c, gx, (gy + d) % 16), tile)
    message[2] = tile
    twin_copy = pltpu.make_async_remote_copy(
        src_ref=message.at[2], dst_ref=twin_in, send_sem=red_send.at[2, 0], recv_sem=red_recv.at[2, 0],
        device_id=(other, gx, gy), device_id_type=MESH)
    twin_copy.start()
    twin_copy.wait_recv()
    tile = tile + twin_in[...]

    square = jnp.concatenate([tile] + [pltpu.roll(tile, 128 - M * b, 1) for b in range(1, 4)], axis=0)
    flipped = jnp.transpose(jnp.concatenate([square, jnp.zeros((96, 128), F32)], axis=0))[0:M]
    upper = li >= ri
    system = jnp.where(upper, square, flipped) + jnp.where(li == ri, M - 1.0, 0.0)
    drive_col = jnp.sum(jnp.where((li == ri + 1), flipped, 0.0), axis=1, keepdims=True)
    last = jnp.sum(jnp.where((ri == 2) & (li == 0), square, 0.0))
    drive_col = jnp.where(ri == M - 1, last, drive_col)
    work = jnp.where(li < M, system, 0.0)
    work = jnp.where(li == ri + M, 1.0, work)
    work = jnp.where(li == 2 * M, drive_col, work)
    done_rows, done_pivots = [], []
    rest = work
    for base in range(0, M, 8):
        height = M - base
        cols = [jnp.broadcast_to(rest[:, base + j:base + j + 1], (height, 128)) for j in range(8)]
        index = lax.broadcasted_iota(jnp.int32, (height, 128), 0)
        pivots = jnp.ones((8, 128), F32)
        for j in range(8):
            pivot = cols[j][j:j + 1, :]
            ratio = jnp.where(index > j, cols[j] * (1.0 / pivot), 0.0)
            pivots = jnp.where(index[0:8] == j, pivot, pivots)
            rest = rest - ratio * rest[j:j + 1, :]
            for i in range(j + 1, 8):
                cols[i] = cols[i] - ratio * cols[i][j:j + 1, :]
        done_rows.append(rest[0:8])
        done_pivots.append(pivots)
        rest = rest[8:]
    work = jnp.concatenate(done_rows, axis=0)
    pivots = jnp.concatenate(done_pivots, axis=0)
    scaled = work * lax.rsqrt(pivots)
    inverse = jnp.where((li >= M) & (li < 2 * M), scaled, 0.0)
    reduced = jnp.sum(jnp.where(li == 2 * M, scaled, 0.0), axis=1, keepdims=True)
    mean_weights = jnp.sum(inverse * reduced, axis=0, keepdims=True)
    combined = math.sqrt(M - 1.0) * inverse + mean_weights
    average = jnp.sum(combined, axis=1, keepdims=True) * (1.0 / M)
    mix_out[...] = combined - average + 1.0 / M

    for k in range(CHUNKS):
        swap_copy(k).wait_send()
        for variable in range(2):
            guarded([row_copy(0, variable, k), row_copy(1, variable, k)],
                    has_next_x, has_last_x, lambda copy: copy.wait_send())
        guarded([row2_copy(0, k), row2_copy(1, k)], has_next_x, has_last_x, lambda copy: copy.wait_send())
        guarded(col_copies(1, k * QC, QC, 1 + k), has_next_y, has_last_y, lambda copy: copy.wait_send())
    guarded(first_cols, has_next_y, has_last_y, lambda copy: copy.wait_send())

    def drain(d, carry):
        plane_copy(d).wait_send()
        line_copy(d).wait_send()
        return carry

    lax.fori_loop(1, 16, drain, 0)
    twin_copy.wait_send()


def mix_kernel(mix, high, low, out, stage, sems):
    spread = (lax.broadcasted_iota(jnp.int32, (128, 256), 0)
              == lax.broadcasted_iota(jnp.int32, (128, 256), 1) // CX + M)
    spread = jnp.where(spread, 1.0, 0.0).astype(BF16)
    wide = sum(jnp.dot(part.astype(BF16), spread, preferred_element_type=F32) for part in split3(mix[...]))
    wide = jnp.broadcast_to(wide[:, None, :], (M, CX, 256)).reshape(256, 256)
    same = (lax.broadcasted_iota(jnp.int32, (256, 256), 0) % CX
            == lax.broadcasted_iota(jnp.int32, (256, 256), 1) % CX)
    mix_hi, mix_lo = split2(jnp.where(same, wide, 0.0))
    dot = functools.partial(jnp.dot, preferred_element_type=F32)

    def put(p):
        return pltpu.make_async_copy(stage.at[p], out.at[0, :, pl.ds(2 * p, 2)], sems.at[p])

    for p in range(LEV // 2):
        hi = jnp.concatenate([high[2 * p], high[2 * p + 1]], axis=1)
        lo = jnp.concatenate([low[2 * p], low[2 * p + 1]], axis=1)
        mixed = dot(mix_hi, hi) + dot(mix_hi, lo) + dot(mix_lo, hi)
        for d in range(2):
            stage[p, :, d] = mixed[:, d * CY:(d + 1) * CY].reshape(M, CX, CY)
        put(p).start()
    for p in range(LEV // 2):
        put(p).wait()


def shards(prior, zonal, meridional, diffusive, column, layer, kind, readings, precision):
    obs = [x.reshape(32, 128) for x in (column, layer, kind, readings, precision)]
    anywhere = pl.BlockSpec(memory_space=pltpu.MemorySpace.HBM)
    inside = pl.BlockSpec(memory_space=pltpu.VMEM)
    high, low, mix = pl.pallas_call(
        forecast_kernel,
        out_shape=(
            pltpu.VMEM((LEV, M * CX, CY), BF16),
            pltpu.VMEM((LEV, M * CX, CY), BF16),
            pltpu.VMEM((M, 128), F32),
        ),
        in_specs=[anywhere] * 9,
        out_specs=(inside, inside, inside),
        scratch_shapes=[
            pltpu.VMEM((M, LEV, CX + 2, CY), F32),
            pltpu.VMEM((M, LEV, CX + 2, CY), F32),
            pltpu.VMEM((5, LEV, CX, CY), F32),
            pltpu.VMEM((3, LEV, CX, CY), F32),
            pltpu.VMEM((3, 32, 128), jnp.int32),
            pltpu.VMEM((8, 32, 128), F32),
            pltpu.VMEM((768, 128), F32),
            pltpu.VMEM((2, LEV, CX, CY), F32),
            pltpu.VMEM((2, 8, CX, CY), F32),
            pltpu.VMEM((2, 8, CX, CY), F32),
            pltpu.VMEM((2, 8, CX, CY), F32),
            pltpu.VMEM((M * CX, CY), F32),
            pltpu.VMEM((272, 256), F32),
            pltpu.VMEM((3, 8, 128), F32),
            pltpu.VMEM((16, 8, 128), F32),
            pltpu.VMEM((16, 8, 128), F32),
            pltpu.VMEM((8, 128), F32),
            pltpu.SemaphoreType.DMA((9,)),
            pltpu.SemaphoreType.DMA((2, 2, CHUNKS)),
            pltpu.SemaphoreType.DMA((2, 2, CHUNKS)),
            pltpu.SemaphoreType.DMA((CHUNKS,)),
            pltpu.SemaphoreType.DMA((CHUNKS,)),
            pltpu.SemaphoreType.DMA((2, 1 + CHUNKS)),
            pltpu.SemaphoreType.DMA((2, 1 + CHUNKS)),
            pltpu.SemaphoreType.DMA((2, CHUNKS)),
            pltpu.SemaphoreType.DMA((2, CHUNKS)),
            pltpu.SemaphoreType.DMA((3, 16)),
            pltpu.SemaphoreType.DMA((3, 16)),
            pltpu.SemaphoreType.REGULAR((3,)),
        ],
        compiler_params=pltpu.CompilerParams(
            collective_id=0, has_side_effects=True, vmem_limit_bytes=64880000),
        name="forecast",
    )(prior, zonal, meridional, diffusive, *obs)
    return pl.pallas_call(
        mix_kernel,
        out_shape=jax.ShapeDtypeStruct((1, M, LEV, CX, CY), F32),
        in_specs=[inside] * 3,
        out_specs=anywhere,
        scratch_shapes=[
            pltpu.VMEM((LEV // 2, M, 2, CX, CY), F32),
            pltpu.SemaphoreType.DMA((LEV // 2,)),
        ],
        compiler_params=pltpu.CompilerParams(vmem_limit_bytes=16 << 20),
        name="mix",
    )(mix, high, low)


def solution(mesh):
    obs = P(("gx", "gy"))
    flow = P(None, "gx", "gy")
    return jax.shard_map(
        shards,
        mesh=mesh,
        in_specs=(P("member", None, None, "gx", "gy"), flow, flow, flow, obs, obs, obs, obs, obs),
        out_specs=P("member", None, None, "gx", "gy"),
        check_vma=False,
    )
```

```python
import functools
import math

import jax
import jax.numpy as jnp
from jax import lax
from jax.experimental import pallas as pl
from jax.experimental.pallas import tpu as pltpu
from jax.sharding import PartitionSpec as P

MESH = pl.DeviceIdType.MESH
F32 = jnp.float32
BF16 = jnp.bfloat16
M, LEV, CX, CY = 32, 16, 8, 128
MID = 8
TOP, BOTTOM, PITCH = MID - 1, MID + CX, 24
HALF = M // 2
CHUNKS = 4
LC = LEV // CHUNKS
QC = LC // 2
NT = (((1,), (1,)), ((), ()))


def split2(x):
    hi = x.astype(BF16)
    lo = (x - hi.astype(F32)).astype(BF16)
    return hi, lo


def split3(x):
    hi = x.astype(BF16).astype(F32)
    mid = (x - hi).astype(BF16).astype(F32)
    return hi, mid, x - hi - mid


def forecast_kernel(
    prior, zonal, meridional, diffusive, column, layer, kind, readings, precision,
    high, low, mix_out,
    z0, z1, coef, flow, obs_i, obs_f, hist, weight, packed, west_in, east_in,
    field, quad, message, plane, line, twin_in,
    local_sem, row_send, row_recv, swap_send, swap_recv, col_send, col_recv,
    row2_send, row2_recv, red_send, red_recv, news,
):
    c = lax.axis_index("member")
    gx = lax.axis_index("gx")
    gy = lax.axis_index("gy")
    other = 1 - c
    mine = pl.multiple_of(c * HALF, HALF)

    local = [pltpu.make_async_copy(prior.at[:, c], z0.at[pl.ds(mine, HALF), :, pl.ds(MID, CX), :], local_sem.at[0])]
    for i, ref in enumerate((zonal, meridional, diffusive)):
        local.append(pltpu.make_async_copy(ref, flow.at[i], local_sem.at[1 + i]))
    for i, ref in enumerate((column, layer, kind)):
        local.append(pltpu.make_async_copy(ref, obs_i.at[i], local_sem.at[4 + i]))
    for i, ref in enumerate((readings, precision)):
        local.append(pltpu.make_async_copy(ref, obs_f.at[i], local_sem.at[7 + i]))
    for copy in local:
        copy.start()

    barrier = pltpu.get_barrier_semaphore()
    def ring_peers(distance):
        return [(c, (gx + distance) % 16, gy), (c, (gx + 16 - distance) % 16, gy),
                (c, gx, (gy + distance) % 16), (c, gx, (gy + 16 - distance) % 16)]

    greet = [(other, gx, gy), (other, (gx + 1) % 16, gy), (other, (gx + 15) % 16, gy)] + ring_peers(1)
    for peer in greet:
        pl.semaphore_signal(barrier, inc=1, device_id=peer, device_id_type=MESH)
    pl.semaphore_wait(barrier, len(greet))

    def tell(stage):
        for peer in ring_peers(2 ** stage):
            pl.semaphore_signal(news.at[stage], inc=1, device_id=peer, device_id_type=MESH)

    def hear(stage):
        pl.semaphore_wait(news.at[stage], 4)

    def row_copy(side, variable, k):
        source_row = CX - 1 if side == 0 else 0
        target_row = TOP if side == 0 else BOTTOM
        target = gx + 1 if side == 0 else gx - 1
        return pltpu.make_async_remote_copy(
            src_ref=prior.at[:, variable, pl.ds(k * LC, LC), source_row, :],
            dst_ref=z0.at[pl.ds(mine, HALF), pl.ds(k * LC, LC), target_row, :],
            send_sem=row_send.at[side, variable, k],
            recv_sem=row_recv.at[side, c, k],
            device_id=(variable, target, gy),
            device_id_type=MESH,
        )

    def row_arrival(side, source, k):
        target_row = TOP if side == 0 else BOTTOM
        here = z0.at[pl.ds(source * HALF, HALF), pl.ds(k * LC, LC), target_row, :]
        return pltpu.make_async_remote_copy(
            src_ref=here, dst_ref=here, send_sem=row_send.at[side, source, k],
            recv_sem=row_recv.at[side, source, k], device_id=(other, gx, gy), device_id_type=MESH,
        )

    def swap_copy(k):
        return pltpu.make_async_remote_copy(
            src_ref=prior.at[:, other, pl.ds(k * LC, LC)],
            dst_ref=z0.at[pl.ds(mine, HALF), pl.ds(k * LC, LC), pl.ds(MID, CX), :],
            send_sem=swap_send.at[k], recv_sem=swap_recv.at[k],
            device_id=(other, gx, gy), device_id_type=MESH,
        )

    def swap_arrival(k):
        here = z0.at[pl.ds(pl.multiple_of(other * HALF, HALF), HALF), pl.ds(k * LC, LC), pl.ds(MID, CX), :]
        return pltpu.make_async_remote_copy(
            src_ref=here, dst_ref=here, send_sem=swap_send.at[k], recv_sem=swap_recv.at[k],
            device_id=(other, gx, gy), device_id_type=MESH,
        )

    for k in range(CHUNKS):
        swap_copy(k).start()
    for k in range(CHUNKS):
        for variable in range(2):
            @pl.when(gx < 15)
            def _():
                row_copy(0, variable, k).start()

            @pl.when(gx > 0)
            def _():
                row_copy(1, variable, k).start()

    tell(0)

    zero_rows = jnp.zeros((M, LEV, CY), F32)
    zero_cols = jnp.zeros((8, CX, CY), F32)

    @pl.when(gx == 0)
    def _():
        z0[:, :, TOP, :] = zero_rows
        z1[:, :, TOP, :] = zero_rows

    @pl.when(gx == 15)
    def _():
        z0[:, :, BOTTOM, :] = zero_rows
        z1[:, :, BOTTOM, :] = zero_rows

    @pl.when(gy == 0)
    def _():
        west_in[0] = zero_cols
        west_in[1] = zero_cols

    @pl.when(gy == 15)
    def _():
        east_in[0] = zero_cols
        east_in[1] = zero_cols

    for copy in local[4:]:
        copy.wait()
    cell = obs_i[0]
    spot_a = obs_i[1] * CX + cell // 2048 - gx * CX
    spot_b = cell % 2048 - gy * CY
    kept = jnp.where(obs_i[2] == c, obs_f[1], 0.0)
    obs_i[0] = spot_a
    obs_i[1] = spot_b
    for i, part in enumerate(split3(kept) + split3(kept * obs_f[0])):
        obs_f[2 + i] = part
    hist[...] = jnp.zeros_like(hist)
    rows_iota = lax.broadcasted_iota(jnp.int32, (128, 128), 0)

    def scatter(i, carry):
        lefts, rights = [], []
        for j in range(2):
            r = 2 * i + j
            in_row = rows_iota == obs_i[0, pl.ds(r, 1), :]
            in_col = rows_iota == obs_i[1, pl.ds(r, 1), :]
            lefts.append(jnp.concatenate(
                [jnp.where(in_row, obs_f[2 + p, pl.ds(r, 1), :], 0.0).astype(BF16) for p in range(6)], axis=0))
            rights.append(jnp.where(in_col, 1.0, 0.0).astype(BF16))
        hist[...] += lax.dot_general(
            jnp.concatenate(lefts, axis=1), jnp.concatenate(rights, axis=1), NT, preferred_element_type=F32)
        return carry

    lax.fori_loop(0, 8, scatter, 0)

    for copy in local[1:4]:
        copy.wait()
    zon, mer, dif = flow[0], flow[1], flow[2]
    east = dif + jnp.maximum(-zon, 0.0)
    west = dif + jnp.maximum(zon, 0.0)
    north = dif + jnp.maximum(-mer, 0.0)
    south = dif + jnp.maximum(mer, 0.0)
    coef[0] = 1.0 - (east + west + north + south)
    coef[1] = east
    coef[2] = west
    coef[3] = north
    coef[4] = south

    lanes = lax.broadcasted_iota(jnp.int32, (CX, CY), 1)
    pair = lanes // 2

    def pack(acc, tile, t):
        return jnp.where(pair == t, pltpu.roll(tile, 2 * t + 1, 1), acc)

    def col_copies(stage, first, count, slot):
        out = []
        for side in range(2):
            target = gy + 1 if side == 0 else gy - 1
            into = west_in if side == 0 else east_in
            out.append(pltpu.make_async_remote_copy(
                src_ref=packed.at[stage, pl.ds(first, count)],
                dst_ref=into.at[stage, pl.ds(first, count)],
                send_sem=col_send.at[side, slot], recv_sem=col_recv.at[side, slot],
                device_id=(c, gx, target), device_id_type=MESH,
            ))
        return out

    def guarded(copies, low_ok, high_ok, act):
        for copy, ok in zip(copies, (low_ok, high_ok)):
            @pl.when(ok)
            def _():
                act(copy)

    has_next_y, has_last_y = gy < 15, gy > 0
    has_next_x, has_last_x = gx < 15, gx > 0

    local[0].wait()
    for k in range(CHUNKS):
        swap_arrival(k).wait_recv()

    def pack_first(q, carry):
        acc = jnp.zeros((CX, CY), F32)
        for d in range(2):
            for m in range(M):
                acc = pack(acc, z0[m, 2 * q + d, MID:BOTTOM, :], d * M + m)
        packed[0, q] = acc
        return carry

    lax.fori_loop(0, 8, pack_first, 0)
    first_cols = col_copies(0, 0, 8, 0)
    guarded(first_cols, has_next_y, has_last_y, lambda copy: copy.start())
    hear(0)
    tell(1)
    lax.fori_loop(8, 16, scatter, 0)
    for i in range(2):
        base = 384 * i
        total = hist[base:base + 128] + hist[base + 128:base + 256] + hist[base + 256:base + 384]
        weight[i] = total.reshape(LEV, CX, CY)
    guarded(first_cols, has_last_y, has_next_y, lambda copy: copy.wait_recv())

    odd = lanes % 2 == 1

    def merge(stage, q):
        return jnp.where(odd, pltpu.roll(west_in[stage, q], 1, 1), pltpu.roll(east_in[stage, q], 127, 1))

    def stencil(src, m, l, t, cols, co):
        edge = pltpu.roll(cols, 127 - 2 * t, 1)
        centre = src[m, l, MID:BOTTOM, :]
        left = jnp.where(lanes == 0, edge, pltpu.roll(centre, 1, 1))
        right = jnp.where(lanes == CY - 1, edge, pltpu.roll(centre, 127, 1))
        return (co[0] * centre + co[1] * src[m, l, MID + 1:BOTTOM + 1, :] + co[2] * src[m, l, TOP:BOTTOM - 1, :]
                + co[3] * right + co[4] * left)

    def row2_copy(side, k):
        source_row = BOTTOM - 1 if side == 0 else MID
        target_row = TOP if side == 0 else BOTTOM
        target = gx + 1 if side == 0 else gx - 1
        return pltpu.make_async_remote_copy(
            src_ref=z1.at[:, pl.ds(k * LC, LC), source_row, :],
            dst_ref=z1.at[:, pl.ds(k * LC, LC), target_row, :],
            send_sem=row2_send.at[side, k], recv_sem=row2_recv.at[side, k],
            device_id=(c, target, gy), device_id_type=MESH,
        )

    def step_one(q, carry):
        cols = merge(0, q)
        acc = jnp.zeros((CX, CY), F32)
        for d in range(2):
            l = 2 * q + d
            co = [coef[i, l] for i in range(5)]
            for m in range(M):
                new = stencil(z0, m, l, d * M + m, cols, co)
                z1[m, l, MID:BOTTOM, :] = new
        for d in range(2):
            for m in range(M):
                acc = pack(acc, z1[m, 2 * q + d, MID:BOTTOM, :], d * M + m)
        packed[1, q] = acc
        return carry

    for k in range(CHUNKS):
        for source in range(2):
            guarded([row_arrival(0, source, k), row_arrival(1, source, k)],
                    has_last_x, has_next_x, lambda copy: copy.wait_recv())
        lax.fori_loop(k * QC, (k + 1) * QC, step_one, 0)
        if k == 1:
            hear(1)
            tell(2)
        guarded([row2_copy(0, k), row2_copy(1, k)], has_next_x, has_last_x, lambda copy: copy.start())
        guarded(col_copies(1, k * QC, QC, 1 + k), has_next_y, has_last_y, lambda copy: copy.start())

    quad[...] = jnp.zeros_like(quad)

    def step_two(q, carry):
        cols = merge(1, q)
        lefts, rights = [], []
        for d in range(2):
            l = 2 * q + d
            co = [coef[i, l] for i in range(5)]
            total = jnp.zeros((CX, CY), F32)
            for m in range(M):
                new = stencil(z1, m, l, d * M + m, cols, co)
                field[m * CX:(m + 1) * CX, :] = new
                total = total + new
            mean = total * (1.0 / M)
            state = field[...]
            hi, lo = split2(state)
            high[l] = hi
            low[l] = lo
            part = (state.reshape(M, CX, CY) - mean[None])
            w = weight[0, l]
            rights.append(part.reshape(M * CX, CY))
            innov = weight[1, l] - w * mean
            lefts.append(jnp.concatenate(
                [(part * w[None]).reshape(M * CX, CY), innov, jnp.zeros((CX, CY), F32)], axis=0))
        left_hi, left_lo = split2(jnp.concatenate(lefts, axis=1))
        right_hi, right_lo = split2(jnp.concatenate(rights, axis=1))
        dot = functools.partial(lax.dot_general, dimension_numbers=NT, preferred_element_type=F32)
        quad[...] += dot(left_hi, right_hi) + dot(left_hi, right_lo) + dot(left_lo, right_hi)
        return carry

    for k in range(CHUNKS):
        guarded([row2_copy(0, k), row2_copy(1, k)], has_last_x, has_next_x, lambda copy: copy.wait_recv())
        guarded(col_copies(1, k * QC, QC, 1 + k), has_last_y, has_next_y, lambda copy: copy.wait_recv())
        lax.fori_loop(k * QC, (k + 1) * QC, step_two, 0)

    hear(2)

    row_x = lax.broadcasted_iota(jnp.int32, (272, 256), 0) % CX
    col_x = lax.broadcasted_iota(jnp.int32, (272, 256), 1) % CX
    kept_terms = jnp.where(row_x == col_x, quad[...], 0.0)
    fold = (lax.broadcasted_iota(jnp.int32, (256, 128), 0) // CX
            == lax.broadcasted_iota(jnp.int32, (256, 128), 1) % M)
    fold = jnp.where(fold, 1.0, 0.0).astype(BF16)
    summed = sum(jnp.dot(part.astype(BF16), fold, preferred_element_type=F32) for part in split3(kept_terms))
    summed = jnp.sum(summed.reshape(34, CX, 128), axis=1)
    gram = summed[0:M]
    drive = summed[M:M + 1]
    ri = lax.broadcasted_iota(jnp.int32, (M, 128), 0)
    li = lax.broadcasted_iota(jnp.int32, (M, 128), 1)
    ci = li % M
    folded = jnp.where(ci >= ri, gram, jnp.where(ci == ri - 1, drive, 0.0))
    folded = jnp.where((ri == 2) & (ci == 0), pltpu.roll(drive, 1, 1), folded)
    block = lanes // M
    tile = jnp.zeros((8, 128), F32)
    for b in range(4):
        tile = jnp.where(block == b, folded[8 * b:8 * b + 8], tile)

    def gather_sum(stage, buffer, peer_of, tile):
        message[stage] = tile

        def copy_of(d):
            return pltpu.make_async_remote_copy(
                src_ref=message.at[stage], dst_ref=buffer.at[d],
                send_sem=red_send.at[stage, d], recv_sem=red_recv.at[stage, d],
                device_id=peer_of(d), device_id_type=MESH,
            )

        def start(d, carry):
            copy_of(d).start()
            return carry

        def finish(d, carry):
            copy_of(d).wait_recv()
            return carry

        lax.fori_loop(1, 16, start, 0)
        lax.fori_loop(1, 16, finish, 0)
        total = tile
        for d in range(1, 16):
            total = total + buffer[d]
        return total, copy_of

    tile, plane_copy = gather_sum(0, plane, lambda d: (c, (gx + d) % 16, gy), tile)
    tile, line_copy = gather_sum(1, line, lambda d: (c, gx, (gy + d) % 16), tile)
    message[2] = tile
    twin_copy = pltpu.make_async_remote_copy(
        src_ref=message.at[2], dst_ref=twin_in, send_sem=red_send.at[2, 0], recv_sem=red_recv.at[2, 0],
        device_id=(other, gx, gy), device_id_type=MESH)
    twin_copy.start()
    twin_copy.wait_recv()
    tile = tile + twin_in[...]

    square = jnp.concatenate([tile] + [pltpu.roll(tile, 128 - M * b, 1) for b in range(1, 4)], axis=0)
    flipped = jnp.transpose(jnp.concatenate([square, jnp.zeros((96, 128), F32)], axis=0))[0:M]
    upper = li >= ri
    system = jnp.where(upper, square, flipped) + jnp.where(li == ri, M - 1.0, 0.0)
    drive_col = jnp.sum(jnp.where((li == ri + 1), flipped, 0.0), axis=1, keepdims=True)
    last = jnp.sum(jnp.where((ri == 2) & (li == 0), square, 0.0))
    drive_col = jnp.where(ri == M - 1, last, drive_col)
    work = jnp.where(li < M, system, 0.0)
    work = jnp.where(li == ri + M, 1.0, work)
    work = jnp.where(li == 2 * M, drive_col, work)
    done_rows, done_pivots = [], []
    rest = work
    for base in range(0, M, 8):
        height = M - base
        cols = [jnp.broadcast_to(rest[:, base + j:base + j + 1], (height, 128)) for j in range(8)]
        index = lax.broadcasted_iota(jnp.int32, (height, 128), 0)
        pivots = jnp.ones((8, 128), F32)
        for j in range(8):
            pivot = cols[j][j:j + 1, :]
            ratio = jnp.where(index > j, cols[j] * (1.0 / pivot), 0.0)
            pivots = jnp.where(index[0:8] == j, pivot, pivots)
            rest = rest - ratio * rest[j:j + 1, :]
            for i in range(j + 1, 8):
                cols[i] = cols[i] - ratio * cols[i][j:j + 1, :]
        done_rows.append(rest[0:8])
        done_pivots.append(pivots)
        rest = rest[8:]
    work = jnp.concatenate(done_rows, axis=0)
    pivots = jnp.concatenate(done_pivots, axis=0)
    scaled = work * lax.rsqrt(pivots)
    inverse = jnp.where((li >= M) & (li < 2 * M), scaled, 0.0)
    reduced = jnp.sum(jnp.where(li == 2 * M, scaled, 0.0), axis=1, keepdims=True)
    mean_weights = jnp.sum(inverse * reduced, axis=0, keepdims=True)
    combined = math.sqrt(M - 1.0) * inverse + mean_weights
    average = jnp.sum(combined, axis=1, keepdims=True) * (1.0 / M)
    mix_out[...] = combined - average + 1.0 / M

    for k in range(CHUNKS):
        swap_copy(k).wait_send()
        for variable in range(2):
            guarded([row_copy(0, variable, k), row_copy(1, variable, k)],
                    has_next_x, has_last_x, lambda copy: copy.wait_send())
        guarded([row2_copy(0, k), row2_copy(1, k)], has_next_x, has_last_x, lambda copy: copy.wait_send())
        guarded(col_copies(1, k * QC, QC, 1 + k), has_next_y, has_last_y, lambda copy: copy.wait_send())
    guarded(first_cols, has_next_y, has_last_y, lambda copy: copy.wait_send())

    def drain(d, carry):
        plane_copy(d).wait_send()
        line_copy(d).wait_send()
        return carry

    lax.fori_loop(1, 16, drain, 0)
    twin_copy.wait_send()


def mix_kernel(mix, high, low, out, stage, sems):
    spread = (lax.broadcasted_iota(jnp.int32, (128, 256), 0)
              == lax.broadcasted_iota(jnp.int32, (128, 256), 1) // CX + M)
    spread = jnp.where(spread, 1.0, 0.0).astype(BF16)
    wide = sum(jnp.dot(part.astype(BF16), spread, preferred_element_type=F32) for part in split3(mix[...]))
    wide = jnp.broadcast_to(wide[:, None, :], (M, CX, 256)).reshape(256, 256)
    same = (lax.broadcasted_iota(jnp.int32, (256, 256), 0) % CX
            == lax.broadcasted_iota(jnp.int32, (256, 256), 1) % CX)
    mix_hi, mix_lo = split2(jnp.where(same, wide, 0.0))
    dot = functools.partial(jnp.dot, preferred_element_type=F32)

    def put(p):
        return pltpu.make_async_copy(stage.at[p], out.at[0, :, pl.ds(2 * p, 2)], sems.at[p])

    for p in range(LEV // 2):
        hi = jnp.concatenate([high[2 * p], high[2 * p + 1]], axis=1)
        lo = jnp.concatenate([low[2 * p], low[2 * p + 1]], axis=1)
        mixed = dot(mix_hi, hi) + dot(mix_hi, lo) + dot(mix_lo, hi)
        for d in range(2):
            stage[p, :, d] = mixed[:, d * CY:(d + 1) * CY].reshape(M, CX, CY)
        put(p).start()
    for p in range(LEV // 2):
        put(p).wait()


def shards(prior, zonal, meridional, diffusive, column, layer, kind, readings, precision):
    obs = [x.reshape(32, 128) for x in (column, layer, kind, readings, precision)]
    anywhere = pl.BlockSpec(memory_space=pltpu.MemorySpace.HBM)
    inside = pl.BlockSpec(memory_space=pltpu.VMEM)
    high, low, mix = pl.pallas_call(
        forecast_kernel,
        out_shape=(
            pltpu.VMEM((LEV, M * CX, CY), BF16),
            pltpu.VMEM((LEV, M * CX, CY), BF16),
            pltpu.VMEM((M, 128), F32),
        ),
        in_specs=[anywhere] * 9,
        out_specs=(inside, inside, inside),
        scratch_shapes=[
            pltpu.VMEM((M, LEV, PITCH, CY), F32),
            pltpu.VMEM((M, LEV, PITCH, CY), F32),
            pltpu.VMEM((5, LEV, CX, CY), F32),
            pltpu.VMEM((3, LEV, CX, CY), F32),
            pltpu.VMEM((3, 32, 128), jnp.int32),
            pltpu.VMEM((8, 32, 128), F32),
            pltpu.VMEM((768, 128), F32),
            pltpu.VMEM((2, LEV, CX, CY), F32),
            pltpu.VMEM((2, 8, CX, CY), F32),
            pltpu.VMEM((2, 8, CX, CY), F32),
            pltpu.VMEM((2, 8, CX, CY), F32),
            pltpu.VMEM((M * CX, CY), F32),
            pltpu.VMEM((272, 256), F32),
            pltpu.VMEM((3, 8, 128), F32),
            pltpu.VMEM((16, 8, 128), F32),
            pltpu.VMEM((16, 8, 128), F32),
            pltpu.VMEM((8, 128), F32),
            pltpu.SemaphoreType.DMA((9,)),
            pltpu.SemaphoreType.DMA((2, 2, CHUNKS)),
            pltpu.SemaphoreType.DMA((2, 2, CHUNKS)),
            pltpu.SemaphoreType.DMA((CHUNKS,)),
            pltpu.SemaphoreType.DMA((CHUNKS,)),
            pltpu.SemaphoreType.DMA((2, 1 + CHUNKS)),
            pltpu.SemaphoreType.DMA((2, 1 + CHUNKS)),
            pltpu.SemaphoreType.DMA((2, CHUNKS)),
            pltpu.SemaphoreType.DMA((2, CHUNKS)),
            pltpu.SemaphoreType.DMA((3, 16)),
            pltpu.SemaphoreType.DMA((3, 16)),
            pltpu.SemaphoreType.REGULAR((3,)),
        ],
        compiler_params=pltpu.CompilerParams(
            collective_id=0, has_side_effects=True, vmem_limit_bytes=64880000),
        name="forecast",
    )(prior, zonal, meridional, diffusive, *obs)
    return pl.pallas_call(
        mix_kernel,
        out_shape=jax.ShapeDtypeStruct((1, M, LEV, CX, CY), F32),
        in_specs=[inside] * 3,
        out_specs=anywhere,
        scratch_shapes=[
            pltpu.VMEM((LEV // 2, M, 2, CX, CY), F32),
            pltpu.SemaphoreType.DMA((LEV // 2,)),
        ],
        compiler_params=pltpu.CompilerParams(vmem_limit_bytes=16 << 20),
        name="mix",
    )(mix, high, low)


def solution(mesh):
    obs = P(("gx", "gy"))
    flow = P(None, "gx", "gy")
    return jax.shard_map(
        shards,
        mesh=mesh,
        in_specs=(P("member", None, None, "gx", "gy"), flow, flow, flow, obs, obs, obs, obs, obs),
        out_specs=P("member", None, None, "gx", "gy"),
        check_vma=False,
    )
```

```python
import functools
import math

import jax
import jax.numpy as jnp
from jax import lax
from jax.experimental import pallas as pl
from jax.experimental.pallas import tpu as pltpu
from jax.sharding import PartitionSpec as P

MESH = pl.DeviceIdType.MESH
F32 = jnp.float32
BF16 = jnp.bfloat16
M, LEV, CX, CY = 32, 16, 8, 128
MID = 8
TOP, BOTTOM, PITCH = MID - 1, MID + CX, 24
HALF = M // 2
CHUNKS = 4
LC = LEV // CHUNKS
QC = LC // 2
NT = (((1,), (1,)), ((), ()))


def split2(x):
    hi = x.astype(BF16)
    lo = (x - hi.astype(F32)).astype(BF16)
    return hi, lo


def split3(x):
    hi = x.astype(BF16).astype(F32)
    mid = (x - hi).astype(BF16).astype(F32)
    return hi, mid, x - hi - mid


def forecast_kernel(
    prior, zonal, meridional, diffusive, column, layer, kind, readings, precision,
    high, low, mix_out,
    z0, z1, coef, flow, obs_i, obs_f, hist, weight, packed, west_in, east_in,
    field, quad, message, plane, line, twin_in,
    local_sem, row_send, row_recv, swap_sem, col_send, col_recv,
    row2_send, row2_recv, red_send, red_recv, news,
):
    c = lax.axis_index("member")
    gx = lax.axis_index("gx")
    gy = lax.axis_index("gy")
    other = 1 - c
    mine = pl.multiple_of(c * HALF, HALF)

    local = [pltpu.make_async_copy(prior.at[:, c], z0.at[pl.ds(mine, HALF), :, pl.ds(MID, CX), :], local_sem.at[0])]
    for i, ref in enumerate((zonal, meridional, diffusive)):
        local.append(pltpu.make_async_copy(ref, flow.at[i], local_sem.at[1 + i]))
    for i, ref in enumerate((column, layer, kind)):
        local.append(pltpu.make_async_copy(ref, obs_i.at[i], local_sem.at[4 + i]))
    for i, ref in enumerate((readings, precision)):
        local.append(pltpu.make_async_copy(ref, obs_f.at[i], local_sem.at[7 + i]))
    for copy in local:
        copy.start()

    barrier = pltpu.get_barrier_semaphore()
    def ring_peers(distance):
        return [(c, (gx + distance) % 16, gy), (c, (gx + 16 - distance) % 16, gy),
                (c, gx, (gy + distance) % 16), (c, gx, (gy + 16 - distance) % 16)]

    greet = [(other, gx, gy), (other, (gx + 1) % 16, gy), (other, (gx + 15) % 16, gy)] + ring_peers(1)
    for peer in greet:
        pl.semaphore_signal(barrier, inc=1, device_id=peer, device_id_type=MESH)
    pl.semaphore_wait(barrier, len(greet))

    def tell(stage):
        for peer in ring_peers(2 ** stage):
            pl.semaphore_signal(news.at[stage], inc=1, device_id=peer, device_id_type=MESH)

    def hear(stage):
        pl.semaphore_wait(news.at[stage], 4)

    def row_copy(side, variable, k):
        source_row = CX - 1 if side == 0 else 0
        target_row = TOP if side == 0 else BOTTOM
        target = gx + 1 if side == 0 else gx - 1
        return pltpu.make_async_remote_copy(
            src_ref=prior.at[:, variable, pl.ds(k * LC, LC), source_row, :],
            dst_ref=z0.at[pl.ds(mine, HALF), pl.ds(k * LC, LC), target_row, :],
            send_sem=row_send.at[side],
            recv_sem=row_recv.at[side, k],
            device_id=(variable, target, gy),
            device_id_type=MESH,
        )

    def row_arrival(side, k):
        here = z0.at[:, pl.ds(k * LC, LC), TOP if side == 0 else BOTTOM, :]
        return pltpu.make_async_remote_copy(
            src_ref=here, dst_ref=here, send_sem=row_send.at[side],
            recv_sem=row_recv.at[side, k], device_id=(other, gx, gy), device_id_type=MESH,
        )

    def rows_sent(side, buffer, sems):
        here = buffer.at[:, :, TOP if side == 0 else BOTTOM, :]
        return pltpu.make_async_remote_copy(
            src_ref=here, dst_ref=here, send_sem=sems.at[side],
            recv_sem=row_recv.at[side, 0], device_id=(other, gx, gy), device_id_type=MESH,
        )

    swap_copy = pltpu.make_async_remote_copy(
        src_ref=prior.at[:, other],
        dst_ref=z0.at[pl.ds(mine, HALF), :, pl.ds(MID, CX), :],
        send_sem=swap_sem.at[0], recv_sem=swap_sem.at[1],
        device_id=(other, gx, gy), device_id_type=MESH,
    )
    swapped = z0.at[pl.ds(pl.multiple_of(other * HALF, HALF), HALF), :, pl.ds(MID, CX), :]
    swap_arrival = pltpu.make_async_remote_copy(
        src_ref=swapped, dst_ref=swapped, send_sem=swap_sem.at[0], recv_sem=swap_sem.at[1],
        device_id=(other, gx, gy), device_id_type=MESH,
    )
    swap_copy.start()
    for k in range(CHUNKS):
        for variable in range(2):
            @pl.when(gx < 15)
            def _():
                row_copy(0, variable, k).start()

            @pl.when(gx > 0)
            def _():
                row_copy(1, variable, k).start()

    tell(0)

    zero_rows = jnp.zeros((M, LEV, CY), F32)
    zero_cols = jnp.zeros((8, CX, CY), F32)

    @pl.when(gx == 0)
    def _():
        z0[:, :, TOP, :] = zero_rows
        z1[:, :, TOP, :] = zero_rows

    @pl.when(gx == 15)
    def _():
        z0[:, :, BOTTOM, :] = zero_rows
        z1[:, :, BOTTOM, :] = zero_rows

    @pl.when(gy == 0)
    def _():
        west_in[0] = zero_cols
        west_in[1] = zero_cols

    @pl.when(gy == 15)
    def _():
        east_in[0] = zero_cols
        east_in[1] = zero_cols

    for copy in local[4:]:
        copy.wait()
    cell = obs_i[0]
    spot_a = obs_i[1] * CX + cell // 2048 - gx * CX
    spot_b = cell % 2048 - gy * CY
    kept = jnp.where(obs_i[2] == c, obs_f[1], 0.0)
    obs_i[0] = spot_a
    obs_i[1] = spot_b
    for i, part in enumerate(split3(kept) + split3(kept * obs_f[0])):
        obs_f[2 + i] = part
    hist[...] = jnp.zeros_like(hist)
    rows_iota = lax.broadcasted_iota(jnp.int32, (128, 128), 0)

    def scatter(i, carry):
        lefts, rights = [], []
        for j in range(2):
            r = 2 * i + j
            in_row = rows_iota == obs_i[0, pl.ds(r, 1), :]
            in_col = rows_iota == obs_i[1, pl.ds(r, 1), :]
            lefts.append(jnp.concatenate(
                [jnp.where(in_row, obs_f[2 + p, pl.ds(r, 1), :], 0.0).astype(BF16) for p in range(6)], axis=0))
            rights.append(jnp.where(in_col, 1.0, 0.0).astype(BF16))
        hist[...] += lax.dot_general(
            jnp.concatenate(lefts, axis=1), jnp.concatenate(rights, axis=1), NT, preferred_element_type=F32)
        return carry

    lax.fori_loop(0, 8, scatter, 0)

    for copy in local[1:4]:
        copy.wait()
    zon, mer, dif = flow[0], flow[1], flow[2]
    east = dif + jnp.maximum(-zon, 0.0)
    west = dif + jnp.maximum(zon, 0.0)
    north = dif + jnp.maximum(-mer, 0.0)
    south = dif + jnp.maximum(mer, 0.0)
    coef[0] = 1.0 - (east + west + north + south)
    coef[1] = east
    coef[2] = west
    coef[3] = north
    coef[4] = south

    lanes = lax.broadcasted_iota(jnp.int32, (CX, CY), 1)
    pair = lanes // 2

    def pack(acc, tile, t):
        return jnp.where(pair == t, pltpu.roll(tile, 2 * t + 1, 1), acc)

    def col_copies(stage, first, count, slot):
        out = []
        for side in range(2):
            target = gy + 1 if side == 0 else gy - 1
            into = west_in if side == 0 else east_in
            out.append(pltpu.make_async_remote_copy(
                src_ref=packed.at[stage, pl.ds(first, count)],
                dst_ref=into.at[stage, pl.ds(first, count)],
                send_sem=col_send.at[side, stage], recv_sem=col_recv.at[side, slot],
                device_id=(c, gx, target), device_id_type=MESH,
            ))
        return out

    def guarded(copies, low_ok, high_ok, act):
        for copy, ok in zip(copies, (low_ok, high_ok)):
            @pl.when(ok)
            def _():
                act(copy)

    has_next_y, has_last_y = gy < 15, gy > 0
    has_next_x, has_last_x = gx < 15, gx > 0

    local[0].wait()
    swap_arrival.wait_recv()

    def pack_first(q, carry):
        acc = jnp.zeros((CX, CY), F32)
        for d in range(2):
            for m in range(M):
                acc = pack(acc, z0[m, 2 * q + d, MID:BOTTOM, :], d * M + m)
        packed[0, q] = acc
        return carry

    lax.fori_loop(0, 8, pack_first, 0)
    first_cols = col_copies(0, 0, 8, 0)
    guarded(first_cols, has_next_y, has_last_y, lambda copy: copy.start())
    hear(0)
    tell(1)
    lax.fori_loop(8, 16, scatter, 0)
    for i in range(2):
        base = 384 * i
        total = hist[base:base + 128] + hist[base + 128:base + 256] + hist[base + 256:base + 384]
        weight[i] = total.reshape(LEV, CX, CY)
    guarded(first_cols, has_last_y, has_next_y, lambda copy: copy.wait_recv())

    odd = lanes % 2 == 1

    def merge(stage, q):
        return jnp.where(odd, pltpu.roll(west_in[stage, q], 1, 1), pltpu.roll(east_in[stage, q], 127, 1))

    def stencil(src, m, l, t, cols, co):
        edge = pltpu.roll(cols, 127 - 2 * t, 1)
        centre = src[m, l, MID:BOTTOM, :]
        left = jnp.where(lanes == 0, edge, pltpu.roll(centre, 1, 1))
        right = jnp.where(lanes == CY - 1, edge, pltpu.roll(centre, 127, 1))
        return (co[0] * centre + co[1] * src[m, l, MID + 1:BOTTOM + 1, :] + co[2] * src[m, l, TOP:BOTTOM - 1, :]
                + co[3] * right + co[4] * left)

    def row2_copy(side, k):
        source_row = BOTTOM - 1 if side == 0 else MID
        target_row = TOP if side == 0 else BOTTOM
        target = gx + 1 if side == 0 else gx - 1
        return pltpu.make_async_remote_copy(
            src_ref=z1.at[:, pl.ds(k * LC, LC), source_row, :],
            dst_ref=z1.at[:, pl.ds(k * LC, LC), target_row, :],
            send_sem=row2_send.at[side], recv_sem=row2_recv.at[side, k],
            device_id=(c, target, gy), device_id_type=MESH,
        )

    def step_one(q, carry):
        cols = merge(0, q)
        acc = jnp.zeros((CX, CY), F32)
        for d in range(2):
            l = 2 * q + d
            co = [coef[i, l] for i in range(5)]
            for m in range(M):
                new = stencil(z0, m, l, d * M + m, cols, co)
                z1[m, l, MID:BOTTOM, :] = new
        for d in range(2):
            for m in range(M):
                acc = pack(acc, z1[m, 2 * q + d, MID:BOTTOM, :], d * M + m)
        packed[1, q] = acc
        return carry

    for k in range(CHUNKS):
        guarded([row_arrival(0, k), row_arrival(1, k)], has_last_x, has_next_x, lambda copy: copy.wait_recv())
        lax.fori_loop(k * QC, (k + 1) * QC, step_one, 0)
        if k == 1:
            hear(1)
            tell(2)
        guarded([row2_copy(0, k), row2_copy(1, k)], has_next_x, has_last_x, lambda copy: copy.start())
        guarded(col_copies(1, k * QC, QC, 1 + k), has_next_y, has_last_y, lambda copy: copy.start())

    quad[...] = jnp.zeros_like(quad)

    def step_two(q, carry):
        cols = merge(1, q)
        lefts, rights = [], []
        for d in range(2):
            l = 2 * q + d
            co = [coef[i, l] for i in range(5)]
            total = jnp.zeros((CX, CY), F32)
            for m in range(M):
                new = stencil(z1, m, l, d * M + m, cols, co)
                field[m * CX:(m + 1) * CX, :] = new
                total = total + new
            mean = total * (1.0 / M)
            state = field[...]
            hi, lo = split2(state)
            high[l] = hi
            low[l] = lo
            part = (state.reshape(M, CX, CY) - mean[None])
            w = weight[0, l]
            rights.append(part.reshape(M * CX, CY))
            innov = weight[1, l] - w * mean
            lefts.append(jnp.concatenate(
                [(part * w[None]).reshape(M * CX, CY), innov, jnp.zeros((CX, CY), F32)], axis=0))
        left_hi, left_lo = split2(jnp.concatenate(lefts, axis=1))
        right_hi, right_lo = split2(jnp.concatenate(rights, axis=1))
        dot = functools.partial(lax.dot_general, dimension_numbers=NT, preferred_element_type=F32)
        quad[...] += dot(left_hi, right_hi) + dot(left_hi, right_lo) + dot(left_lo, right_hi)
        return carry

    for k in range(CHUNKS):
        guarded([row2_copy(0, k), row2_copy(1, k)], has_last_x, has_next_x, lambda copy: copy.wait_recv())
        guarded(col_copies(1, k * QC, QC, 1 + k), has_last_y, has_next_y, lambda copy: copy.wait_recv())
        lax.fori_loop(k * QC, (k + 1) * QC, step_two, 0)

    hear(2)

    row_x = lax.broadcasted_iota(jnp.int32, (272, 256), 0) % CX
    col_x = lax.broadcasted_iota(jnp.int32, (272, 256), 1) % CX
    kept_terms = jnp.where(row_x == col_x, quad[...], 0.0)
    fold = (lax.broadcasted_iota(jnp.int32, (256, 128), 0) // CX
            == lax.broadcasted_iota(jnp.int32, (256, 128), 1) % M)
    fold = jnp.where(fold, 1.0, 0.0).astype(BF16)
    summed = sum(jnp.dot(part.astype(BF16), fold, preferred_element_type=F32) for part in split3(kept_terms))
    summed = jnp.sum(summed.reshape(34, CX, 128), axis=1)
    gram = summed[0:M]
    drive = summed[M:M + 1]
    ri = lax.broadcasted_iota(jnp.int32, (M, 128), 0)
    li = lax.broadcasted_iota(jnp.int32, (M, 128), 1)
    ci = li % M
    folded = jnp.where(ci >= ri, gram, jnp.where(ci == ri - 1, drive, 0.0))
    folded = jnp.where((ri == 2) & (ci == 0), pltpu.roll(drive, 1, 1), folded)
    block = lanes // M
    tile = jnp.zeros((8, 128), F32)
    for b in range(4):
        tile = jnp.where(block == b, folded[8 * b:8 * b + 8], tile)

    def gather_sum(stage, buffer, peer_of, tile):
        message[stage] = tile

        def copy_of(d):
            return pltpu.make_async_remote_copy(
                src_ref=message.at[stage], dst_ref=buffer.at[d],
                send_sem=red_send.at[stage], recv_sem=red_recv.at[stage],
                device_id=peer_of(d), device_id_type=MESH,
            )

        def start(d, carry):
            copy_of(d).start()
            return carry

        slots = buffer.at[pl.ds(1, 15)]
        every = pltpu.make_async_remote_copy(
            src_ref=slots, dst_ref=slots, send_sem=red_send.at[stage], recv_sem=red_recv.at[stage],
            device_id=(other, gx, gy), device_id_type=MESH,
        )
        lax.fori_loop(1, 16, start, 0)
        every.wait_recv()
        total = tile
        for d in range(1, 16):
            total = total + buffer[d]
        return total, every

    tile, plane_all = gather_sum(0, plane, lambda d: (c, (gx + d) % 16, gy), tile)
    tile, line_all = gather_sum(1, line, lambda d: (c, gx, (gy + d) % 16), tile)
    message[2] = tile
    twin_copy = pltpu.make_async_remote_copy(
        src_ref=message.at[2], dst_ref=twin_in, send_sem=red_send.at[2], recv_sem=red_recv.at[2],
        device_id=(other, gx, gy), device_id_type=MESH)
    twin_copy.start()
    twin_copy.wait_recv()
    tile = tile + twin_in[...]

    square = jnp.concatenate([tile] + [pltpu.roll(tile, 128 - M * b, 1) for b in range(1, 4)], axis=0)
    flipped = jnp.transpose(jnp.concatenate([square, jnp.zeros((96, 128), F32)], axis=0))[0:M]
    upper = li >= ri
    system = jnp.where(upper, square, flipped) + jnp.where(li == ri, M - 1.0, 0.0)
    drive_col = jnp.sum(jnp.where((li == ri + 1), flipped, 0.0), axis=1, keepdims=True)
    last = jnp.sum(jnp.where((ri == 2) & (li == 0), square, 0.0))
    drive_col = jnp.where(ri == M - 1, last, drive_col)
    work = jnp.where(li < M, system, 0.0)
    work = jnp.where(li == ri + M, 1.0, work)
    work = jnp.where(li == 2 * M, drive_col, work)
    done_rows, done_pivots = [], []
    rest = work
    for base in range(0, M, 8):
        height = M - base
        cols = [jnp.broadcast_to(rest[:, base + j:base + j + 1], (height, 128)) for j in range(8)]
        index = lax.broadcasted_iota(jnp.int32, (height, 128), 0)
        pivots = jnp.ones((8, 128), F32)
        for j in range(8):
            pivot = cols[j][j:j + 1, :]
            ratio = jnp.where(index > j, cols[j] * (1.0 / pivot), 0.0)
            pivots = jnp.where(index[0:8] == j, pivot, pivots)
            rest = rest - ratio * rest[j:j + 1, :]
            for i in range(j + 1, 8):
                cols[i] = cols[i] - ratio * cols[i][j:j + 1, :]
        done_rows.append(rest[0:8])
        done_pivots.append(pivots)
        rest = rest[8:]
    work = jnp.concatenate(done_rows, axis=0)
    pivots = jnp.concatenate(done_pivots, axis=0)
    scaled = work * lax.rsqrt(pivots)
    inverse = jnp.where((li >= M) & (li < 2 * M), scaled, 0.0)
    reduced = jnp.sum(jnp.where(li == 2 * M, scaled, 0.0), axis=1, keepdims=True)
    mean_weights = jnp.sum(inverse * reduced, axis=0, keepdims=True)
    combined = math.sqrt(M - 1.0) * inverse + mean_weights
    average = jnp.sum(combined, axis=1, keepdims=True) * (1.0 / M)
    mix_out[...] = combined - average + 1.0 / M

    swap_copy.wait_send()
    for buffer, sems in ((z0, row_send), (z1, row2_send)):
        guarded([rows_sent(0, buffer, sems), rows_sent(1, buffer, sems)],
                has_next_x, has_last_x, lambda copy: copy.wait_send())
    for stage in range(2):
        guarded(col_copies(stage, 0, 8, 0), has_next_y, has_last_y, lambda copy: copy.wait_send())
    plane_all.wait_send()
    line_all.wait_send()
    twin_copy.wait_send()


def mix_kernel(mix, high, low, out, stage, sems):
    spread = (lax.broadcasted_iota(jnp.int32, (128, 256), 0)
              == lax.broadcasted_iota(jnp.int32, (128, 256), 1) // CX + M)
    spread = jnp.where(spread, 1.0, 0.0).astype(BF16)
    wide = sum(jnp.dot(part.astype(BF16), spread, preferred_element_type=F32) for part in split3(mix[...]))
    wide = jnp.broadcast_to(wide[:, None, :], (M, CX, 256)).reshape(256, 256)
    same = (lax.broadcasted_iota(jnp.int32, (256, 256), 0) % CX
            == lax.broadcasted_iota(jnp.int32, (256, 256), 1) % CX)
    mix_hi, mix_lo = split2(jnp.where(same, wide, 0.0))
    dot = functools.partial(jnp.dot, preferred_element_type=F32)

    def put(p):
        return pltpu.make_async_copy(stage.at[p], out.at[0, :, pl.ds(2 * p, 2)], sems.at[p])

    for p in range(LEV // 2):
        hi = jnp.concatenate([high[2 * p], high[2 * p + 1]], axis=1)
        lo = jnp.concatenate([low[2 * p], low[2 * p + 1]], axis=1)
        mixed = dot(mix_hi, hi) + dot(mix_hi, lo) + dot(mix_lo, hi)
        for d in range(2):
            stage[p, :, d] = mixed[:, d * CY:(d + 1) * CY].reshape(M, CX, CY)
        put(p).start()
    for p in range(LEV // 2):
        put(p).wait()


def shards(prior, zonal, meridional, diffusive, column, layer, kind, readings, precision):
    obs = [x.reshape(32, 128) for x in (column, layer, kind, readings, precision)]
    anywhere = pl.BlockSpec(memory_space=pltpu.MemorySpace.HBM)
    inside = pl.BlockSpec(memory_space=pltpu.VMEM)
    high, low, mix = pl.pallas_call(
        forecast_kernel,
        out_shape=(
            pltpu.VMEM((LEV, M * CX, CY), BF16),
            pltpu.VMEM((LEV, M * CX, CY), BF16),
            pltpu.VMEM((M, 128), F32),
        ),
        in_specs=[anywhere] * 9,
        out_specs=(inside, inside, inside),
        scratch_shapes=[
            pltpu.VMEM((M, LEV, PITCH, CY), F32),
            pltpu.VMEM((M, LEV, PITCH, CY), F32),
            pltpu.VMEM((5, LEV, CX, CY), F32),
            pltpu.VMEM((3, LEV, CX, CY), F32),
            pltpu.VMEM((3, 32, 128), jnp.int32),
            pltpu.VMEM((8, 32, 128), F32),
            pltpu.VMEM((768, 128), F32),
            pltpu.VMEM((2, LEV, CX, CY), F32),
            pltpu.VMEM((2, 8, CX, CY), F32),
            pltpu.VMEM((2, 8, CX, CY), F32),
            pltpu.VMEM((2, 8, CX, CY), F32),
            pltpu.VMEM((M * CX, CY), F32),
            pltpu.VMEM((272, 256), F32),
            pltpu.VMEM((3, 8, 128), F32),
            pltpu.VMEM((16, 8, 128), F32),
            pltpu.VMEM((16, 8, 128), F32),
            pltpu.VMEM((8, 128), F32),
            pltpu.SemaphoreType.DMA((9,)),
            pltpu.SemaphoreType.DMA((2,)),
            pltpu.SemaphoreType.DMA((2, CHUNKS)),
            pltpu.SemaphoreType.DMA((2,)),
            pltpu.SemaphoreType.DMA((2, 2)),
            pltpu.SemaphoreType.DMA((2, 1 + CHUNKS)),
            pltpu.SemaphoreType.DMA((2,)),
            pltpu.SemaphoreType.DMA((2, CHUNKS)),
            pltpu.SemaphoreType.DMA((3,)),
            pltpu.SemaphoreType.DMA((3,)),
            pltpu.SemaphoreType.REGULAR((3,)),
        ],
        compiler_params=pltpu.CompilerParams(
            collective_id=0, has_side_effects=True, vmem_limit_bytes=64880000),
        name="forecast",
    )(prior, zonal, meridional, diffusive, *obs)
    return pl.pallas_call(
        mix_kernel,
        out_shape=jax.ShapeDtypeStruct((1, M, LEV, CX, CY), F32),
        in_specs=[inside] * 3,
        out_specs=anywhere,
        scratch_shapes=[
            pltpu.VMEM((LEV // 2, M, 2, CX, CY), F32),
            pltpu.SemaphoreType.DMA((LEV // 2,)),
        ],
        compiler_params=pltpu.CompilerParams(vmem_limit_bytes=16 << 20),
        name="mix",
    )(mix, high, low)


def solution(mesh):
    obs = P(("gx", "gy"))
    flow = P(None, "gx", "gy")
    return jax.shard_map(
        shards,
        mesh=mesh,
        in_specs=(P("member", None, None, "gx", "gy"), flow, flow, flow, obs, obs, obs, obs, obs),
        out_specs=P("member", None, None, "gx", "gy"),
        check_vma=False,
    )
```

```python
import functools
import math

import jax
import jax.numpy as jnp
from jax import lax
from jax.experimental import pallas as pl
from jax.experimental.pallas import tpu as pltpu
from jax.sharding import PartitionSpec as P

MESH = pl.DeviceIdType.MESH
F32 = jnp.float32
BF16 = jnp.bfloat16
M, LEV, CX, CY = 32, 16, 8, 128
MID = 8
TOP, BOTTOM, PITCH = MID - 1, MID + CX, 24
HALF = M // 2
CHUNKS = 4
LC = LEV // CHUNKS
QC = LC // 2
FAR_IN_PLANE = (10, 9, 11, 6, 14, 5, 7, 13, 15, 2, 8, 1, 3, 4, 12)
FAR_IN_LINE = (8, 7, 9, 6, 10, 5, 11, 4, 12, 3, 13, 2, 14, 1, 15)
NT = (((1,), (1,)), ((), ()))


def split2(x):
    hi = x.astype(BF16)
    lo = (x - hi.astype(F32)).astype(BF16)
    return hi, lo


def split3(x):
    hi = x.astype(BF16).astype(F32)
    mid = (x - hi).astype(BF16).astype(F32)
    return hi, mid, x - hi - mid


def forecast_kernel(
    prior, zonal, meridional, diffusive, column, layer, kind, readings, precision,
    high, low, mix_out,
    z0, z1, coef, flow, obs_i, obs_f, hist, weight, packed, west_in, east_in,
    field, quad, message, plane, line, twin_in,
    local_sem, row_send, row_recv, swap_sem, col_send, col_recv,
    row2_send, row2_recv, red_send, red_recv, news,
):
    c = lax.axis_index("member")
    gx = lax.axis_index("gx")
    gy = lax.axis_index("gy")
    other = 1 - c
    mine = pl.multiple_of(c * HALF, HALF)

    local = [pltpu.make_async_copy(prior.at[:, c], z0.at[pl.ds(mine, HALF), :, pl.ds(MID, CX), :], local_sem.at[0])]
    for i, ref in enumerate((zonal, meridional, diffusive)):
        local.append(pltpu.make_async_copy(ref, flow.at[i], local_sem.at[1 + i]))
    for i, ref in enumerate((column, layer, kind)):
        local.append(pltpu.make_async_copy(ref, obs_i.at[i], local_sem.at[4 + i]))
    for i, ref in enumerate((readings, precision)):
        local.append(pltpu.make_async_copy(ref, obs_f.at[i], local_sem.at[7 + i]))
    for copy in local:
        copy.start()

    barrier = pltpu.get_barrier_semaphore()
    def ring_peers(distance):
        return [(c, (gx + distance) % 16, gy), (c, (gx + 16 - distance) % 16, gy),
                (c, gx, (gy + distance) % 16), (c, gx, (gy + 16 - distance) % 16)]

    greet = [(other, gx, gy), (other, (gx + 1) % 16, gy), (other, (gx + 15) % 16, gy)] + ring_peers(1)
    for peer in greet:
        pl.semaphore_signal(barrier, inc=1, device_id=peer, device_id_type=MESH)
    pl.semaphore_wait(barrier, len(greet))

    def tell(stage):
        for peer in ring_peers(2 ** stage):
            pl.semaphore_signal(news.at[stage], inc=1, device_id=peer, device_id_type=MESH)

    def hear(stage):
        pl.semaphore_wait(news.at[stage], 4)

    def row_copy(side, variable, k):
        source_row = CX - 1 if side == 0 else 0
        target_row = TOP if side == 0 else BOTTOM
        target = gx + 1 if side == 0 else gx - 1
        return pltpu.make_async_remote_copy(
            src_ref=prior.at[:, variable, pl.ds(k * LC, LC), source_row, :],
            dst_ref=z0.at[pl.ds(mine, HALF), pl.ds(k * LC, LC), target_row, :],
            send_sem=row_send.at[side],
            recv_sem=row_recv.at[side, k],
            device_id=(variable, target, gy),
            device_id_type=MESH,
        )

    def row_arrival(side, k):
        here = z0.at[:, pl.ds(k * LC, LC), TOP if side == 0 else BOTTOM, :]
        return pltpu.make_async_remote_copy(
            src_ref=here, dst_ref=here, send_sem=row_send.at[side],
            recv_sem=row_recv.at[side, k], device_id=(other, gx, gy), device_id_type=MESH,
        )

    def rows_sent(side, buffer, sems):
        here = buffer.at[:, :, TOP if side == 0 else BOTTOM, :]
        return pltpu.make_async_remote_copy(
            src_ref=here, dst_ref=here, send_sem=sems.at[side],
            recv_sem=row_recv.at[side, 0], device_id=(other, gx, gy), device_id_type=MESH,
        )

    swap_copy = pltpu.make_async_remote_copy(
        src_ref=prior.at[:, other],
        dst_ref=z0.at[pl.ds(mine, HALF), :, pl.ds(MID, CX), :],
        send_sem=swap_sem.at[0], recv_sem=swap_sem.at[1],
        device_id=(other, gx, gy), device_id_type=MESH,
    )
    swapped = z0.at[pl.ds(pl.multiple_of(other * HALF, HALF), HALF), :, pl.ds(MID, CX), :]
    swap_arrival = pltpu.make_async_remote_copy(
        src_ref=swapped, dst_ref=swapped, send_sem=swap_sem.at[0], recv_sem=swap_sem.at[1],
        device_id=(other, gx, gy), device_id_type=MESH,
    )
    swap_copy.start()
    for k in range(CHUNKS):
        for variable in range(2):
            @pl.when(gx < 15)
            def _():
                row_copy(0, variable, k).start()

            @pl.when(gx > 0)
            def _():
                row_copy(1, variable, k).start()

    tell(0)

    zero_rows = jnp.zeros((M, LEV, CY), F32)
    zero_cols = jnp.zeros((8, CX, CY), F32)

    @pl.when(gx == 0)
    def _():
        z0[:, :, TOP, :] = zero_rows
        z1[:, :, TOP, :] = zero_rows

    @pl.when(gx == 15)
    def _():
        z0[:, :, BOTTOM, :] = zero_rows
        z1[:, :, BOTTOM, :] = zero_rows

    @pl.when(gy == 0)
    def _():
        west_in[0] = zero_cols
        west_in[1] = zero_cols

    @pl.when(gy == 15)
    def _():
        east_in[0] = zero_cols
        east_in[1] = zero_cols

    for copy in local[4:]:
        copy.wait()
    cell = obs_i[0]
    spot_a = obs_i[1] * CX + cell // 2048 - gx * CX
    spot_b = cell % 2048 - gy * CY
    kept = jnp.where(obs_i[2] == c, obs_f[1], 0.0)
    obs_i[0] = spot_a
    obs_i[1] = spot_b
    for i, part in enumerate(split3(kept) + split3(kept * obs_f[0])):
        obs_f[2 + i] = part
    hist[...] = jnp.zeros_like(hist)
    rows_iota = lax.broadcasted_iota(jnp.int32, (128, 128), 0)

    def scatter(i, carry):
        lefts, rights = [], []
        for j in range(2):
            r = 2 * i + j
            in_row = rows_iota == obs_i[0, pl.ds(r, 1), :]
            in_col = rows_iota == obs_i[1, pl.ds(r, 1), :]
            lefts.append(jnp.concatenate(
                [jnp.where(in_row, obs_f[2 + p, pl.ds(r, 1), :], 0.0).astype(BF16) for p in range(6)], axis=0))
            rights.append(jnp.where(in_col, 1.0, 0.0).astype(BF16))
        hist[...] += lax.dot_general(
            jnp.concatenate(lefts, axis=1), jnp.concatenate(rights, axis=1), NT, preferred_element_type=F32)
        return carry

    lax.fori_loop(0, 8, scatter, 0)

    for copy in local[1:4]:
        copy.wait()
    zon, mer, dif = flow[0], flow[1], flow[2]
    east = dif + jnp.maximum(-zon, 0.0)
    west = dif + jnp.maximum(zon, 0.0)
    north = dif + jnp.maximum(-mer, 0.0)
    south = dif + jnp.maximum(mer, 0.0)
    coef[0] = 1.0 - (east + west + north + south)
    coef[1] = east
    coef[2] = west
    coef[3] = north
    coef[4] = south

    lanes = lax.broadcasted_iota(jnp.int32, (CX, CY), 1)
    pair = lanes // 2

    def pack(acc, tile, t):
        return jnp.where(pair == t, pltpu.roll(tile, 2 * t + 1, 1), acc)

    def col_copies(stage, first, count, slot):
        out = []
        for side in range(2):
            target = gy + 1 if side == 0 else gy - 1
            into = west_in if side == 0 else east_in
            out.append(pltpu.make_async_remote_copy(
                src_ref=packed.at[stage, pl.ds(first, count)],
                dst_ref=into.at[stage, pl.ds(first, count)],
                send_sem=col_send.at[side, stage], recv_sem=col_recv.at[side, slot],
                device_id=(c, gx, target), device_id_type=MESH,
            ))
        return out

    def guarded(copies, low_ok, high_ok, act):
        for copy, ok in zip(copies, (low_ok, high_ok)):
            @pl.when(ok)
            def _():
                act(copy)

    has_next_y, has_last_y = gy < 15, gy > 0
    has_next_x, has_last_x = gx < 15, gx > 0

    local[0].wait()
    swap_arrival.wait_recv()

    def pack_first(q, carry):
        acc = jnp.zeros((CX, CY), F32)
        for d in range(2):
            for m in range(M):
                acc = pack(acc, z0[m, 2 * q + d, MID:BOTTOM, :], d * M + m)
        packed[0, q] = acc
        return carry

    lax.fori_loop(0, 8, pack_first, 0)
    first_cols = col_copies(0, 0, 8, 0)
    guarded(first_cols, has_next_y, has_last_y, lambda copy: copy.start())
    hear(0)
    tell(1)
    lax.fori_loop(8, 16, scatter, 0)
    for i in range(2):
        base = 384 * i
        total = hist[base:base + 128] + hist[base + 128:base + 256] + hist[base + 256:base + 384]
        weight[i] = total.reshape(LEV, CX, CY)
    guarded(first_cols, has_last_y, has_next_y, lambda copy: copy.wait_recv())

    odd = lanes % 2 == 1

    def merge(stage, q):
        return jnp.where(odd, pltpu.roll(west_in[stage, q], 1, 1), pltpu.roll(east_in[stage, q], 127, 1))

    def stencil(src, m, l, t, cols, co):
        edge = pltpu.roll(cols, 127 - 2 * t, 1)
        centre = src[m, l, MID:BOTTOM, :]
        left = jnp.where(lanes == 0, edge, pltpu.roll(centre, 1, 1))
        right = jnp.where(lanes == CY - 1, edge, pltpu.roll(centre, 127, 1))
        return (co[0] * centre + co[1] * src[m, l, MID + 1:BOTTOM + 1, :] + co[2] * src[m, l, TOP:BOTTOM - 1, :]
                + co[3] * right + co[4] * left)

    def row2_copy(side, k):
        source_row = BOTTOM - 1 if side == 0 else MID
        target_row = TOP if side == 0 else BOTTOM
        target = gx + 1 if side == 0 else gx - 1
        return pltpu.make_async_remote_copy(
            src_ref=z1.at[:, pl.ds(k * LC, LC), source_row, :],
            dst_ref=z1.at[:, pl.ds(k * LC, LC), target_row, :],
            send_sem=row2_send.at[side], recv_sem=row2_recv.at[side, k],
            device_id=(c, target, gy), device_id_type=MESH,
        )

    def step_one(q, carry):
        cols = merge(0, q)
        acc = jnp.zeros((CX, CY), F32)
        for d in range(2):
            l = 2 * q + d
            co = [coef[i, l] for i in range(5)]
            for m in range(M):
                new = stencil(z0, m, l, d * M + m, cols, co)
                z1[m, l, MID:BOTTOM, :] = new
        for d in range(2):
            for m in range(M):
                acc = pack(acc, z1[m, 2 * q + d, MID:BOTTOM, :], d * M + m)
        packed[1, q] = acc
        return carry

    for k in range(CHUNKS):
        guarded([row_arrival(0, k), row_arrival(1, k)], has_last_x, has_next_x, lambda copy: copy.wait_recv())
        lax.fori_loop(k * QC, (k + 1) * QC, step_one, 0)
        if k == 1:
            hear(1)
            tell(2)
        guarded([row2_copy(0, k), row2_copy(1, k)], has_next_x, has_last_x, lambda copy: copy.start())
        guarded(col_copies(1, k * QC, QC, 1 + k), has_next_y, has_last_y, lambda copy: copy.start())

    quad[...] = jnp.zeros_like(quad)

    def step_two(q, carry):
        cols = merge(1, q)
        lefts, rights = [], []
        for d in range(2):
            l = 2 * q + d
            co = [coef[i, l] for i in range(5)]
            total = jnp.zeros((CX, CY), F32)
            for m in range(M):
                new = stencil(z1, m, l, d * M + m, cols, co)
                field[m * CX:(m + 1) * CX, :] = new
                total = total + new
            mean = total * (1.0 / M)
            state = field[...]
            hi, lo = split2(state)
            high[l] = hi
            low[l] = lo
            part = (state.reshape(M, CX, CY) - mean[None])
            w = weight[0, l]
            rights.append(part.reshape(M * CX, CY))
            innov = weight[1, l] - w * mean
            lefts.append(jnp.concatenate(
                [(part * w[None]).reshape(M * CX, CY), innov, jnp.zeros((CX, CY), F32)], axis=0))
        left_hi, left_lo = split2(jnp.concatenate(lefts, axis=1))
        right_hi, right_lo = split2(jnp.concatenate(rights, axis=1))
        dot = functools.partial(lax.dot_general, dimension_numbers=NT, preferred_element_type=F32)
        quad[...] += dot(left_hi, right_hi) + dot(left_hi, right_lo) + dot(left_lo, right_hi)
        return carry

    for k in range(CHUNKS):
        guarded([row2_copy(0, k), row2_copy(1, k)], has_last_x, has_next_x, lambda copy: copy.wait_recv())
        guarded(col_copies(1, k * QC, QC, 1 + k), has_last_y, has_next_y, lambda copy: copy.wait_recv())
        lax.fori_loop(k * QC, (k + 1) * QC, step_two, 0)

    hear(2)

    row_x = lax.broadcasted_iota(jnp.int32, (272, 256), 0) % CX
    col_x = lax.broadcasted_iota(jnp.int32, (272, 256), 1) % CX
    kept_terms = jnp.where(row_x == col_x, quad[...], 0.0)
    fold = (lax.broadcasted_iota(jnp.int32, (256, 128), 0) // CX
            == lax.broadcasted_iota(jnp.int32, (256, 128), 1) % M)
    fold = jnp.where(fold, 1.0, 0.0).astype(BF16)
    summed = sum(jnp.dot(part.astype(BF16), fold, preferred_element_type=F32) for part in split3(kept_terms))
    summed = jnp.sum(summed.reshape(34, CX, 128), axis=1)
    gram = summed[0:M]
    drive = summed[M:M + 1]
    ri = lax.broadcasted_iota(jnp.int32, (M, 128), 0)
    li = lax.broadcasted_iota(jnp.int32, (M, 128), 1)
    ci = li % M
    folded = jnp.where(ci >= ri, gram, jnp.where(ci == ri - 1, drive, 0.0))
    folded = jnp.where((ri == 2) & (ci == 0), pltpu.roll(drive, 1, 1), folded)
    block = lanes // M
    tile = jnp.zeros((8, 128), F32)
    for b in range(4):
        tile = jnp.where(block == b, folded[8 * b:8 * b + 8], tile)

    def gather_sum(stage, buffer, peer_of, order, tile):
        message[stage] = tile

        def copy_of(d):
            return pltpu.make_async_remote_copy(
                src_ref=message.at[stage], dst_ref=buffer.at[d],
                send_sem=red_send.at[stage], recv_sem=red_recv.at[stage],
                device_id=peer_of(d), device_id_type=MESH,
            )

        slots = buffer.at[pl.ds(1, 15)]
        every = pltpu.make_async_remote_copy(
            src_ref=slots, dst_ref=slots, send_sem=red_send.at[stage], recv_sem=red_recv.at[stage],
            device_id=(other, gx, gy), device_id_type=MESH,
        )
        for d in order:
            copy_of(d).start()
        every.wait_recv()
        total = tile
        for d in range(1, 16):
            total = total + buffer[d]
        return total, every

    tile, plane_all = gather_sum(0, plane, lambda d: (c, (gx + d) % 16, gy), FAR_IN_PLANE, tile)
    tile, line_all = gather_sum(1, line, lambda d: (c, gx, (gy + d) % 16), FAR_IN_LINE, tile)
    message[2] = tile
    twin_copy = pltpu.make_async_remote_copy(
        src_ref=message.at[2], dst_ref=twin_in, send_sem=red_send.at[2], recv_sem=red_recv.at[2],
        device_id=(other, gx, gy), device_id_type=MESH)
    twin_copy.start()
    twin_copy.wait_recv()
    tile = tile + twin_in[...]

    square = jnp.concatenate([tile] + [pltpu.roll(tile, 128 - M * b, 1) for b in range(1, 4)], axis=0)
    flipped = jnp.transpose(jnp.concatenate([square, jnp.zeros((96, 128), F32)], axis=0))[0:M]
    upper = li >= ri
    system = jnp.where(upper, square, flipped) + jnp.where(li == ri, M - 1.0, 0.0)
    drive_col = jnp.sum(jnp.where((li == ri + 1), flipped, 0.0), axis=1, keepdims=True)
    last = jnp.sum(jnp.where((ri == 2) & (li == 0), square, 0.0))
    drive_col = jnp.where(ri == M - 1, last, drive_col)
    work = jnp.where(li < M, system, 0.0)
    work = jnp.where(li == ri + M, 1.0, work)
    work = jnp.where(li == 2 * M, drive_col, work)
    done_rows, done_pivots = [], []
    rest = work
    for base in range(0, M, 8):
        height = M - base
        cols = [jnp.broadcast_to(rest[:, base + j:base + j + 1], (height, 128)) for j in range(8)]
        index = lax.broadcasted_iota(jnp.int32, (height, 128), 0)
        pivots = jnp.ones((8, 128), F32)
        for j in range(8):
            pivot = cols[j][j:j + 1, :]
            ratio = jnp.where(index > j, cols[j] * (1.0 / pivot), 0.0)
            pivots = jnp.where(index[0:8] == j, pivot, pivots)
            rest = rest - ratio * rest[j:j + 1, :]
            for i in range(j + 1, 8):
                cols[i] = cols[i] - ratio * cols[i][j:j + 1, :]
        done_rows.append(rest[0:8])
        done_pivots.append(pivots)
        rest = rest[8:]
    work = jnp.concatenate(done_rows, axis=0)
    pivots = jnp.concatenate(done_pivots, axis=0)
    scaled = work * lax.rsqrt(pivots)
    inverse = jnp.where((li >= M) & (li < 2 * M), scaled, 0.0)
    reduced = jnp.sum(jnp.where(li == 2 * M, scaled, 0.0), axis=1, keepdims=True)
    mean_weights = jnp.sum(inverse * reduced, axis=0, keepdims=True)
    combined = math.sqrt(M - 1.0) * inverse + mean_weights
    average = jnp.sum(combined, axis=1, keepdims=True) * (1.0 / M)
    mix_out[...] = combined - average + 1.0 / M

    swap_copy.wait_send()
    for buffer, sems in ((z0, row_send), (z1, row2_send)):
        guarded([rows_sent(0, buffer, sems), rows_sent(1, buffer, sems)],
                has_next_x, has_last_x, lambda copy: copy.wait_send())
    for stage in range(2):
        guarded(col_copies(stage, 0, 8, 0), has_next_y, has_last_y, lambda copy: copy.wait_send())
    plane_all.wait_send()
    line_all.wait_send()
    twin_copy.wait_send()


def mix_kernel(mix, high, low, out, stage, sems):
    spread = (lax.broadcasted_iota(jnp.int32, (128, 256), 0)
              == lax.broadcasted_iota(jnp.int32, (128, 256), 1) // CX + M)
    spread = jnp.where(spread, 1.0, 0.0).astype(BF16)
    wide = sum(jnp.dot(part.astype(BF16), spread, preferred_element_type=F32) for part in split3(mix[...]))
    wide = jnp.broadcast_to(wide[:, None, :], (M, CX, 256)).reshape(256, 256)
    same = (lax.broadcasted_iota(jnp.int32, (256, 256), 0) % CX
            == lax.broadcasted_iota(jnp.int32, (256, 256), 1) % CX)
    mix_hi, mix_lo = split2(jnp.where(same, wide, 0.0))
    dot = functools.partial(jnp.dot, preferred_element_type=F32)

    def put(p):
        return pltpu.make_async_copy(stage.at[p], out.at[0, :, pl.ds(2 * p, 2)], sems.at[p])

    for p in range(LEV // 2):
        hi = jnp.concatenate([high[2 * p], high[2 * p + 1]], axis=1)
        lo = jnp.concatenate([low[2 * p], low[2 * p + 1]], axis=1)
        mixed = dot(mix_hi, hi) + dot(mix_hi, lo) + dot(mix_lo, hi)
        for d in range(2):
            stage[p, :, d] = mixed[:, d * CY:(d + 1) * CY].reshape(M, CX, CY)
        put(p).start()
    for p in range(LEV // 2):
        put(p).wait()


def shards(prior, zonal, meridional, diffusive, column, layer, kind, readings, precision):
    obs = [x.reshape(32, 128) for x in (column, layer, kind, readings, precision)]
    anywhere = pl.BlockSpec(memory_space=pltpu.MemorySpace.HBM)
    inside = pl.BlockSpec(memory_space=pltpu.VMEM)
    high, low, mix = pl.pallas_call(
        forecast_kernel,
        out_shape=(
            pltpu.VMEM((LEV, M * CX, CY), BF16),
            pltpu.VMEM((LEV, M * CX, CY), BF16),
            pltpu.VMEM((M, 128), F32),
        ),
        in_specs=[anywhere] * 9,
        out_specs=(inside, inside, inside),
        scratch_shapes=[
            pltpu.VMEM((M, LEV, PITCH, CY), F32),
            pltpu.VMEM((M, LEV, PITCH, CY), F32),
            pltpu.VMEM((5, LEV, CX, CY), F32),
            pltpu.VMEM((3, LEV, CX, CY), F32),
            pltpu.VMEM((3, 32, 128), jnp.int32),
            pltpu.VMEM((8, 32, 128), F32),
            pltpu.VMEM((768, 128), F32),
            pltpu.VMEM((2, LEV, CX, CY), F32),
            pltpu.VMEM((2, 8, CX, CY), F32),
            pltpu.VMEM((2, 8, CX, CY), F32),
            pltpu.VMEM((2, 8, CX, CY), F32),
            pltpu.VMEM((M * CX, CY), F32),
            pltpu.VMEM((272, 256), F32),
            pltpu.VMEM((3, 8, 128), F32),
            pltpu.VMEM((16, 8, 128), F32),
            pltpu.VMEM((16, 8, 128), F32),
            pltpu.VMEM((8, 128), F32),
            pltpu.SemaphoreType.DMA((9,)),
            pltpu.SemaphoreType.DMA((2,)),
            pltpu.SemaphoreType.DMA((2, CHUNKS)),
            pltpu.SemaphoreType.DMA((2,)),
            pltpu.SemaphoreType.DMA((2, 2)),
            pltpu.SemaphoreType.DMA((2, 1 + CHUNKS)),
            pltpu.SemaphoreType.DMA((2,)),
            pltpu.SemaphoreType.DMA((2, CHUNKS)),
            pltpu.SemaphoreType.DMA((3,)),
            pltpu.SemaphoreType.DMA((3,)),
            pltpu.SemaphoreType.REGULAR((3,)),
        ],
        compiler_params=pltpu.CompilerParams(
            collective_id=0, has_side_effects=True, vmem_limit_bytes=64880000),
        name="forecast",
    )(prior, zonal, meridional, diffusive, *obs)
    return pl.pallas_call(
        mix_kernel,
        out_shape=jax.ShapeDtypeStruct((1, M, LEV, CX, CY), F32),
        in_specs=[inside] * 3,
        out_specs=anywhere,
        scratch_shapes=[
            pltpu.VMEM((LEV // 2, M, 2, CX, CY), F32),
            pltpu.SemaphoreType.DMA((LEV // 2,)),
        ],
        compiler_params=pltpu.CompilerParams(vmem_limit_bytes=16 << 20),
        name="mix",
    )(mix, high, low)


def solution(mesh):
    obs = P(("gx", "gy"))
    flow = P(None, "gx", "gy")
    return jax.shard_map(
        shards,
        mesh=mesh,
        in_specs=(P("member", None, None, "gx", "gy"), flow, flow, flow, obs, obs, obs, obs, obs),
        out_specs=P("member", None, None, "gx", "gy"),
        check_vma=False,
    )
```
